128 devices in a mesh: ty: 16 (over x, y), tx: 8 (over z, core).
Axes of the slice: x: 4, y: 4, z: 4, core: 2. Of those that a mesh axis runs over, the one named last changes fastest.
Arguments:
- potential: float32 [4, 4096, 2048], P(None, 'ty', 'tx'), may hold values from -6 to 6
- probe: float32 [2, 256, 256], replicated, may hold values from -4.2 to 4.2
- patterns: bfloat16 [256, 256, 256], P(('ty', 'tx')), may hold values from 0 to 12
- scan_centers: int32 [256, 2], P(('ty', 'tx')), may hold values from 128 to 3967, as said below
Outputs:
- potential_grad: float32 [4, 4096, 2048], P(None, 'ty', 'tx')
The draws below stay inside these ranges and needn't reach their ends.
Inputs may be any that keep to these rules, and one draw needn't show every extreme that they name: `scan_centers`: rows of the device at index i of ty (blocks of 2 rows per device, ty slowest) have their first entry in [i * 256, (i + 1) * 256); the second entries of one device's rows lie in distinct column tiles of 256 cells; in each index of ty some column tile is named by every device of that index; every window of 256 x 256 cells around a centre lies inside the object.
All inputs are finite; a program needn't handle non-finite values.
Results may differ from the reference program's by a relative error of at most 0.035.
The reference program's roundings to bfloat16 on the way count: a program that leaves them out, or rounds other values in their place, can miss the bound.
Values may be sent and summed in bfloat16 or wider, within the bound.
No kernel may reach another device: no remote copies, remote signals or barrier semaphores. Data moves between devices by JAX's collectives and lax.ppermute only.
A program may use at most 128 MiB of HBM per device.

```python
import math
import jax
import jax.numpy as jnp
from jax import lax

WIN = 256
SLICES = 4
TILE_Y = 256
TILE_X = 256
POS_DEV = 2
NY = 4096
NX = 2048
POSITIONS = 256


def draw_patterns(key, part):
    shape = (POSITIONS, WIN, WIN)
    uniform_cells = jax.random.uniform(key, shape, jnp.float32, 1e-07, 1.0)
    values = jnp.minimum(-1.5 * jnp.log(uniform_cells), 12.0)
    return values.astype(jnp.bfloat16)


def draw_scan_centers(key, part):
    tile_rows = NY // TILE_Y
    tile_cols = NX // TILE_X
    devices_all = tile_rows * tile_cols
    half_win = WIN // 2
    subkeys = jax.random.split(key, 4)
    busy_col = jax.random.randint(subkeys[0], (tile_rows,), 0, tile_cols)
    scores = jax.random.randint(subkeys[1], (devices_all, tile_cols), 0, 1 << 20)
    scores = scores * tile_cols + jnp.arange(tile_cols, dtype=jnp.int32)[None, :]
    band_index = jnp.arange(devices_all, dtype=jnp.int32) // tile_cols
    chosen = jnp.arange(tile_cols, dtype=jnp.int32)[None, :] == busy_col[band_index][:, None]
    scores = jnp.where(chosen, -1, scores)
    destinations = jnp.argsort(scores, axis=1)[:, :POS_DEV].astype(jnp.int32)
    low_row = jnp.maximum(band_index * TILE_Y, half_win)
    high_row = jnp.minimum(band_index * TILE_Y + TILE_Y, NY - half_win)
    row_pick = jax.random.randint(subkeys[2], (devices_all, POS_DEV), 0, 1 << 20)
    row_centres = low_row[:, None] + row_pick % (high_row - low_row)[:, None]
    low_col = jnp.maximum(destinations * TILE_X, half_win)
    high_col = jnp.minimum(destinations * TILE_X + TILE_X, NX - half_win)
    col_pick = jax.random.randint(subkeys[3], (devices_all, POS_DEV), 0, 1 << 20)
    col_centres = low_col + col_pick % (high_col - low_col)
    return jnp.stack([row_centres, col_centres], -1).reshape(devices_all * POS_DEV, 2).astype(jnp.int32)


def block_levels(stream_key, extent, cuts, least, largest):
    level = 1.0
    for dim, blocks in cuts:
        draws = jax.random.uniform(jax.random.fold_in(jax.random.fold_in(stream_key, 6), dim), (blocks,), jnp.float32, least / len(cuts), largest / len(cuts))
        level = level * jnp.repeat(jnp.exp(draws), extent[dim] // blocks).reshape((-1,) + (1,) * (len(extent) - 1 - dim))
    return level


def noise(rng, extent, deviation, reach, pieces=(), held_as=jnp.bfloat16):
    factor_of = block_levels(rng, extent, pieces, -0.22, 0.18) if pieces else 1.0
    result = jax.random.normal(rng, extent, jnp.float32) * deviation * factor_of
    return jnp.minimum(jnp.maximum(result, -reach), reach).astype(held_as)


def setup_inputs(seed: int = 0) -> dict:
    arg_keys = jax.random.split(jax.random.key(seed), 5)
    potential = noise(arg_keys[0], (SLICES, NY, NX), 1.0, 6.0, ((1, 16), (2, 8)), jnp.float32)
    probe = noise(arg_keys[1], (2, WIN, WIN), 0.7, 4.2, (), jnp.float32)
    patterns = draw_patterns(jax.random.fold_in(arg_keys[4], 71), 0)
    scan_centers = draw_scan_centers(jax.random.fold_in(arg_keys[4], 71), 0)
    return {"potential": potential, "probe": probe, "patterns": patterns, "scan_centers": scan_centers}


interaction = 0.5
fresnel = 41.0
band_reach = 20.0

def make_tables(length):
    indices = jnp.arange(length, dtype=jnp.int32)
    offset_gap = (indices[:, None] - indices[None, :]).astype(jnp.float32)
    chirp_phase = math.pi * offset_gap * offset_gap / fresnel
    inside = (jnp.abs(offset_gap) <= band_reach).astype(jnp.float32)
    amplitude = inside / math.sqrt(fresnel)
    prop_pair = ((amplitude * jnp.cos(chirp_phase)).astype(jnp.bfloat16), (amplitude * jnp.sin(chirp_phase)).astype(jnp.bfloat16))
    product = indices[:, None] * indices[None, :] % length
    dft_angle = -2.0 * math.pi * product.astype(jnp.float32) / length
    norm_factor = 1.0 / math.sqrt(length)
    four_pair = ((jnp.cos(dft_angle) * norm_factor).astype(jnp.bfloat16), (jnp.sin(dft_angle) * norm_factor).astype(jnp.bfloat16))
    return (prop_pair, four_pair)

def apply_pair(table, real_part, imag_part):
    table_real, table_imag = table
    length = real_part.shape[0]
    left_block = jnp.concatenate([jnp.concatenate([table_real, -table_imag], 1), jnp.concatenate([table_imag, table_real], 1)], 0)
    stacked = jnp.concatenate([real_part, imag_part], 0).astype(jnp.bfloat16)
    middle = jnp.dot(left_block, stacked, preferred_element_type=jnp.float32).astype(jnp.bfloat16)
    first_prod = jnp.dot(middle, table_real.T, preferred_element_type=jnp.float32)
    second_prod = jnp.dot(middle, table_imag.T, preferred_element_type=jnp.float32)
    return (first_prod[:length] - second_prod[length:], second_prod[:length] + first_prod[length:])

def window_loss(window, probe, pattern, operators):
    prop_pair, four_pair = operators
    real_part, imag_part = (probe[0], probe[1])
    count = window.shape[0]
    for slab_index in range(count):
        shift_phase = interaction * window[slab_index]
        cosine, sine_part = (jnp.cos(shift_phase), jnp.sin(shift_phase))
        real_part, imag_part = (real_part * cosine - imag_part * sine_part, real_part * sine_part + imag_part * cosine)
        if slab_index + 1 < count:
            real_part, imag_part = apply_pair(prop_pair, real_part, imag_part)
    real_part, imag_part = apply_pair(four_pair, real_part, imag_part)
    excess = real_part * real_part + imag_part * imag_part - pattern.astype(jnp.float32)
    return 0.5 * jnp.sum(excess * excess)

def reference(potential, probe, patterns, scan_centers):
    operators = make_tables(WIN)
    half_win = WIN // 2
    grad_fn = jax.grad(window_loss)
    corners = (scan_centers - half_win).astype(jnp.int32)
    zero_index = jnp.zeros((), jnp.int32)

    def accumulate(number, running):
        row_at = corners[number, 0]
        col_at = corners[number, 1]
        window = lax.dynamic_slice(potential, (zero_index, row_at, col_at), (SLICES, WIN, WIN))
        window_grad = grad_fn(window, probe, patterns[number], operators)
        current = lax.dynamic_slice(running, (zero_index, row_at, col_at), (SLICES, WIN, WIN))
        return lax.dynamic_update_slice(running, current + window_grad, (zero_index, row_at, col_at))
    return lax.fori_loop(0, corners.shape[0], accumulate, jnp.zeros(potential.shape, jnp.float32))
```

```python
import functools
import math

import jax
import jax.numpy as jnp
import numpy as np
from jax import lax
from jax.experimental import pallas as pl
from jax.experimental.pallas import tpu as pltpu
from jax.sharding import PartitionSpec as P

fresnel = 41.0
band_reach = 20.0
SLOT_PAD = 16
LANES = 128
PITCH = 5


def sin_cos_coefs(limit):
    nodes = np.cos((np.arange(512) + 0.5) * np.pi / 512)
    u = 0.5 * (nodes + 1.0)
    v = np.sqrt(u) * limit
    t = 0.5 * v
    sinc = np.where(t == 0, 0.5, np.sin(t) / np.where(v == 0, 1.0, v))
    scale = limit * limit
    a = np.polynomial.polynomial.polyfit(u, sinc, 6) / scale ** np.arange(7)
    b = np.polynomial.polynomial.polyfit(u, np.cos(t), 7) / scale ** np.arange(8)
    return [float(np.float32(x)) for x in a], [float(np.float32(x)) for x in b]


SIN_COEFS, COS_COEFS = sin_cos_coefs(6.0)


def sin_cos_half(v):
    u = v * v
    s = SIN_COEFS[-1]
    for a in SIN_COEFS[-2::-1]:
        s = s * u + a
    c = COS_COEFS[-1]
    for b in COS_COEFS[-2::-1]:
        c = c * u + b
    return s * v, c


def make_tables(length):
    f32 = np.float32
    indices = np.arange(length, dtype=np.int32)
    gap = (indices[:, None] - indices[None, :]).astype(f32)
    chirp = f32(math.pi) * gap * gap / f32(fresnel)
    amplitude = (np.abs(gap) <= band_reach).astype(f32) / f32(math.sqrt(fresnel))
    product = indices[:, None] * indices[None, :] % length
    angle = f32(-2.0 * math.pi) * product.astype(f32) / f32(length)
    norm = f32(1.0 / math.sqrt(length))
    pairs = [
        (amplitude * np.cos(chirp), amplitude * np.sin(chirp)),
        (np.cos(angle) * norm, np.sin(angle) * norm),
    ]
    tables = []
    for re, im in pairs:
        left = np.block([[re, -im], [im, re]])
        right = np.block([[re, im], [-im, re]])
        tables += [left.astype(jnp.bfloat16), right.astype(jnp.bfloat16)]
    return np.stack(tables)


def windows_kernel(
    half, where_ref, own_ref, up_ref, down_ref, west_ref, east_ref, probe_ref, pat_ref, tab_ref,
    mid_ref, wout_ref, eout_ref,
    ext_ref, acc_ref, cs_ref, phi_ref, s_ref, t_ref,
):
    slices, tile_y, tile_x = own_ref.shape
    width = probe_ref.shape[1]
    slots = pat_ref.shape[0]
    rows = 64
    f32, bf16 = jnp.float32, jnp.bfloat16
    tall = tile_y + width
    blocks = (tile_x + width) // LANES
    side = half // LANES
    halves = width // LANES

    def every(start, count, block):
        return pl.ds(start * PITCH + block, count, stride=PITCH)

    for s in range(slices):
        for b in range(blocks):
            if b < side:
                ext_ref[s, every(0, tall, b)] = west_ref[s, :, b * LANES : (b + 1) * LANES].astype(f32)
            elif b >= blocks - side:
                c = b - (blocks - side)
                ext_ref[s, every(0, tall, b)] = east_ref[s, :, c * LANES : (c + 1) * LANES].astype(f32)
            else:
                c = slice((b - side) * LANES, (b - side + 1) * LANES)
                ext_ref[s, every(0, half, b)] = up_ref[s, :, c].astype(f32)
                ext_ref[s, every(half, tile_y, b)] = own_ref[s, :, c].astype(bf16).astype(f32)
                ext_ref[s, every(half + tile_y, half, b)] = down_ref[s, :, c].astype(f32)
        acc_ref[s] = jnp.zeros(acc_ref.shape[1:], f32)

    def dot(a, b):
        return jnp.dot(a, b, preferred_element_type=f32)

    def chunks():
        return [slice(k * rows, (k + 1) * rows) for k in range(width // rows)]

    def one_window(slot):
        row = where_ref[slot, 0]
        col = where_ref[slot, 1]
        block = col // LANES
        turn = col - block * LANES
        back = jnp.where(turn == 0, 0, LANES - turn)
        lane = lax.broadcasted_iota(jnp.int32, (rows, LANES), 1)
        low = lane < LANES - turn
        high = lane >= turn

        def modulate(s, k, re, im):
            parts = [
                pltpu.roll(ext_ref[s, every(row + k.start, rows, block + j)], back, 1)
                for j in range(halves + 1)
            ]
            for j in range(halves):
                c = slice(j * LANES, (j + 1) * LANES)
                sin, cos = sin_cos_half(jnp.where(low, parts[j], parts[j + 1]))
                cs_ref[s, 0, k, c] = cos
                cs_ref[s, 1, k, c] = sin
                new_re = re[:, c] * cos - im[:, c] * sin
                new_im = re[:, c] * sin + im[:, c] * cos
                phi_ref[s, 0, k, c] = new_re
                phi_ref[s, 1, k, c] = new_im
                s_ref[k, c] = new_re.astype(bf16)
                s_ref[width + k.start : width + k.stop, c] = new_im.astype(bf16)

        def deposit(s, k, grad):
            parts = [pltpu.roll(grad[:, j * LANES : (j + 1) * LANES], turn, 1) for j in range(halves)]
            zero = jnp.zeros((rows, LANES), f32)
            for j in range(halves + 1):
                here = parts[j] if j < halves else zero
                before = parts[j - 1] if j else zero
                acc_ref[s, every(row + k.start, rows, block + j)] += jnp.where(high, here, before)

        def apply(table):
            mid = dot(tab_ref[table], s_ref[...]).astype(bf16)
            t_ref[:, :width] = mid[:width]
            t_ref[:, width:] = mid[width:]
            return dot(t_ref[...], tab_ref[table + 1])

        def apply_back(table):
            mid = dot(t_ref[...], tab_ref[table]).astype(bf16)
            s_ref[:width] = mid[:, :width]
            s_ref[width:] = mid[:, width:]
            return dot(tab_ref[table + 1], s_ref[...])

        for k in chunks():
            modulate(0, k, probe_ref[0, k], probe_ref[1, k])
        for s in range(1, slices):
            z = apply(0)
            for k in chunks():
                modulate(s, k, z[k, :width], z[k, width:])
        z = apply(2)
        for k in chunks():
            re, im = z[k, :width], z[k, width:]
            excess = re * re + im * im - pat_ref[slot, k].astype(f32)
            twice = excess + excess
            t_ref[k, :width] = (twice * re).astype(bf16)
            t_ref[k, width:] = (twice * im).astype(bf16)
        for s in range(slices - 1, -1, -1):
            g = apply_back(2 if s == slices - 1 else 0)
            for k in chunks():
                re, im = g[k], g[width + k.start : width + k.stop]
                grad = 0.5 * (im * phi_ref[s, 0, k] - re * phi_ref[s, 1, k])
                deposit(s, k, grad)
                if s:
                    cos, sin = cs_ref[s, 0, k], cs_ref[s, 1, k]
                    t_ref[k, :width] = (re * cos + im * sin).astype(bf16)
                    t_ref[k, width:] = (im * cos - re * sin).astype(bf16)

    def step(slot, carry):
        @pl.when(where_ref[slot, 2] > 0)
        def _():
            one_window(slot)

        return carry

    lax.fori_loop(0, slots, step, 0)
    for s in range(slices):
        for b in range(blocks):
            part = acc_ref[s, every(0, tall, b)]
            if b < side:
                wout_ref[s, :, b * LANES : (b + 1) * LANES] = part.astype(bf16)
            elif b >= blocks - side:
                c = b - (blocks - side)
                eout_ref[s, :, c * LANES : (c + 1) * LANES] = part.astype(bf16)
            else:
                c = b - side
                mid_ref[s, :, c * LANES : (c + 1) * LANES] = part


def run_windows(where, own, up, down, west, east, probe, patterns, tables, interpret=False):
    slices, tile_y, tile_x = own.shape
    width = probe.shape[1]
    half = width // 2
    tall = tile_y + width
    f32, bf16 = jnp.float32, jnp.bfloat16
    vmem = pl.BlockSpec(memory_space=pltpu.VMEM)
    return pl.pallas_call(
        functools.partial(windows_kernel, half),
        out_shape=(
            jax.ShapeDtypeStruct((slices, tall, tile_x), f32),
            jax.ShapeDtypeStruct((slices, tall, half), bf16),
            jax.ShapeDtypeStruct((slices, tall, half), bf16),
        ),
        in_specs=[pl.BlockSpec(memory_space=pltpu.SMEM)] + [vmem] * 8,
        out_specs=(vmem,) * 3,
        scratch_shapes=[
            pltpu.VMEM((slices, tall * PITCH, LANES), f32),
            pltpu.VMEM((slices, tall * PITCH, LANES), f32),
            pltpu.VMEM((slices, 2, width, width), f32),
            pltpu.VMEM((slices, 2, width, width), f32),
            pltpu.VMEM((2 * width, width), bf16),
            pltpu.VMEM((width, 2 * width), bf16),
        ],
        compiler_params=pltpu.CompilerParams(vmem_limit_bytes=56 << 20),
        interpret=interpret,
    )(where, own, up, down, west, east, probe, patterns, tables)


def shift(cells, axis, step):
    count = lax.axis_size(axis)
    pairs = [(i, i + step) for i in range(count) if 0 <= i + step < count]
    return lax.ppermute(cells, axis, pairs)


def per_device(tables, potential, probe, patterns, scan_centers):
    slices, tile_y, tile_x = potential.shape
    width = probe.shape[1]
    half = width // 2
    columns = lax.axis_size("tx")
    f32, bf16 = jnp.float32, jnp.bfloat16

    owner = scan_centers[:, 1] // tile_x
    rows_local = scan_centers[:, 0] - lax.axis_index("ty") * tile_y
    cols_local = scan_centers[:, 1] - owner * tile_x
    info = jnp.stack([rows_local, cols_local, jnp.ones_like(owner)], -1).astype(bf16)
    info = jnp.pad(info, ((0, 0), (0, width - 3)))[:, None]
    parcels = jnp.concatenate(
        [patterns, jnp.broadcast_to(info, (2, SLOT_PAD, width))], 1
    )
    target = jnp.arange(columns, dtype=jnp.int32)[:, None, None]
    zero = jnp.zeros((), bf16)
    sent = jnp.where(
        owner[0] == target, parcels[0], jnp.where(owner[1] == target, parcels[1], zero)
    )
    got = lax.all_to_all(sent, "tx", split_axis=0, concat_axis=0, tiled=True)
    where = got[:, width, :3].astype(f32).astype(jnp.int32)

    rounded = potential.astype(bf16)
    up = shift(rounded[:, tile_y - half :], "ty", 1)
    down = shift(rounded[:, :half], "ty", -1)

    def strip(cols):
        return jnp.concatenate([up[:, :, cols], rounded[:, :, cols], down[:, :, cols]], 1)

    west = shift(strip(slice(tile_x - half, tile_x)), "tx", 1)
    east = shift(strip(slice(0, half)), "tx", -1)

    mid, to_west, to_east = run_windows(
        where, potential, up, down, west, east, probe, got, tables
    )

    from_west = shift(to_east, "tx", 1)
    from_east = shift(to_west, "tx", -1)

    def with_sides(lo, hi):
        add = jnp.concatenate([from_west[:, lo:hi], from_east[:, lo:hi]], 2)
        return mid[:, lo:hi] + add.astype(f32)

    from_up = shift(with_sides(half + tile_y, 2 * half + tile_y).astype(bf16), "ty", 1)
    from_down = shift(with_sides(0, half).astype(bf16), "ty", -1)
    return with_sides(half, half + tile_y) + jnp.concatenate([from_up, from_down], 1).astype(f32)


def solution(mesh):
    in_specs = (P(None, "ty", "tx"), P(), P(("ty", "tx"), None, None), P(("ty", "tx"), None))
    out_specs = P(None, "ty", "tx")

    def run(potential, probe, patterns, scan_centers):
        tables = jnp.asarray(make_tables(probe.shape[1]))
        return jax.shard_map(
            functools.partial(per_device, tables),
            mesh=mesh, in_specs=in_specs, out_specs=out_specs, check_vma=False,
        )(potential, probe, patterns, scan_centers)

    return run
```

```python
import functools
import math

import jax
import jax.numpy as jnp
import numpy as np
from jax import lax
from jax.experimental import pallas as pl
from jax.experimental.pallas import tpu as pltpu
from jax.sharding import PartitionSpec as P

fresnel = 41.0
band_reach = 20.0
SLOT_PAD = 16
LANES = 128
PITCH = 5


def sin_cos_coefs(limit):
    nodes = np.cos((np.arange(512) + 0.5) * np.pi / 512)
    u = 0.5 * (nodes + 1.0)
    v = np.sqrt(u) * limit
    t = 0.5 * v
    sinc = np.where(t == 0, 0.5, np.sin(t) / np.where(v == 0, 1.0, v))
    scale = limit * limit
    a = np.polynomial.polynomial.polyfit(u, sinc, 6) / scale ** np.arange(7)
    b = np.polynomial.polynomial.polyfit(u, np.cos(t), 7) / scale ** np.arange(8)
    return [float(np.float32(x)) for x in a], [float(np.float32(x)) for x in b]


SIN_COEFS, COS_COEFS = sin_cos_coefs(6.0)


def sin_cos_half(v):
    u = v * v
    s = SIN_COEFS[-1]
    for a in SIN_COEFS[-2::-1]:
        s = s * u + a
    c = COS_COEFS[-1]
    for b in COS_COEFS[-2::-1]:
        c = c * u + b
    return s * v, c


def make_tables(length):
    f32 = np.float32
    indices = np.arange(length, dtype=np.int32)
    gap = (indices[:, None] - indices[None, :]).astype(f32)
    chirp = f32(math.pi) * gap * gap / f32(fresnel)
    amplitude = (np.abs(gap) <= band_reach).astype(f32) / f32(math.sqrt(fresnel))
    product = indices[:, None] * indices[None, :] % length
    angle = f32(-2.0 * math.pi) * product.astype(f32) / f32(length)
    norm = f32(1.0 / math.sqrt(length))
    pairs = [
        (amplitude * np.cos(chirp), amplitude * np.sin(chirp)),
        (np.cos(angle) * norm, np.sin(angle) * norm),
    ]
    tables = []
    for re, im in pairs:
        left = np.block([[re, -im], [im, re]])
        right = np.block([[re, im], [-im, re]])
        tables += [left.astype(jnp.bfloat16), right.astype(jnp.bfloat16)]
    return np.stack(tables)


def windows_kernel(
    half, where_ref, own_ref, up_ref, down_ref, west_ref, east_ref, probe_hbm, pat_ref, tab_hbm,
    mid_ref, wout_ref, eout_ref,
    ext_ref, acc_ref, order_ref, probe_ref, tab_ref, sems, *streams,
):
    loads = [
        pltpu.make_async_copy(tab_hbm, tab_ref, sems.at[0]),
        pltpu.make_async_copy(probe_hbm, probe_ref, sems.at[1]),
    ]
    for load in loads:
        load.start()
    slices, tile_y, tile_x = own_ref.shape
    width = probe_ref.shape[1]
    slots = pat_ref.shape[0]
    rows = 64
    f32, bf16 = jnp.float32, jnp.bfloat16
    tall = tile_y + width
    blocks = (tile_x + width) // LANES
    side = half // LANES
    halves = width // LANES

    def every(start, count, block):
        return pl.ds(start * PITCH + block, count, stride=PITCH)

    for s in range(slices):
        for b in range(blocks):
            if b < side:
                ext_ref[s, every(0, tall, b)] = west_ref[s, :, b * LANES : (b + 1) * LANES].astype(f32)
            elif b >= blocks - side:
                c = b - (blocks - side)
                ext_ref[s, every(0, tall, b)] = east_ref[s, :, c * LANES : (c + 1) * LANES].astype(f32)
            else:
                c = slice((b - side) * LANES, (b - side + 1) * LANES)
                ext_ref[s, every(0, half, b)] = up_ref[s, :, c].astype(f32)
                ext_ref[s, every(half, tile_y, b)] = own_ref[s, :, c].astype(bf16).astype(f32)
                ext_ref[s, every(half + tile_y, half, b)] = down_ref[s, :, c].astype(f32)
        acc_ref[s] = jnp.zeros(acc_ref.shape[1:], f32)
    for load in loads:
        load.wait()

    def dot(a, b):
        return jnp.dot(a, b, preferred_element_type=f32)

    def chunks():
        return [slice(k * rows, (k + 1) * rows) for k in range(width // rows)]

    def one_window(slot, cs_ref, phi_ref, s_ref, t_ref):
        row = where_ref[slot, 0]
        col = where_ref[slot, 1]
        block = col // LANES
        turn = col - block * LANES
        back = jnp.where(turn == 0, 0, LANES - turn)
        lane = lax.broadcasted_iota(jnp.int32, (rows, LANES), 1)
        low = lane < LANES - turn
        high = lane >= turn

        def modulate(s, k, re, im):
            parts = [
                pltpu.roll(ext_ref[s, every(row + k.start, rows, block + j)], back, 1)
                for j in range(halves + 1)
            ]
            for j in range(halves):
                c = slice(j * LANES, (j + 1) * LANES)
                sin, cos = sin_cos_half(jnp.where(low, parts[j], parts[j + 1]))
                cs_ref[s, 0, k, c] = cos
                cs_ref[s, 1, k, c] = sin
                new_re = re[:, c] * cos - im[:, c] * sin
                new_im = re[:, c] * sin + im[:, c] * cos
                phi_ref[s, 0, k, c] = new_re
                phi_ref[s, 1, k, c] = new_im
                s_ref[k, c] = new_re.astype(bf16)
                s_ref[width + k.start : width + k.stop, c] = new_im.astype(bf16)

        def deposit(s, k, grad):
            parts = [pltpu.roll(grad[:, j * LANES : (j + 1) * LANES], turn, 1) for j in range(halves)]
            zero = jnp.zeros((rows, LANES), f32)
            for j in range(halves + 1):
                here = parts[j] if j < halves else zero
                before = parts[j - 1] if j else zero
                acc_ref[s, every(row + k.start, rows, block + j)] += jnp.where(high, here, before)

        def apply(table):
            mid = dot(tab_ref[table], s_ref[...]).astype(bf16)
            t_ref[:, :width] = mid[:width]
            t_ref[:, width:] = mid[width:]
            return dot(t_ref[...], tab_ref[table + 1])

        def apply_back(table):
            mid = dot(t_ref[...], tab_ref[table]).astype(bf16)
            s_ref[:width] = mid[:, :width]
            s_ref[width:] = mid[:, width:]
            return dot(tab_ref[table + 1], s_ref[...])

        for k in chunks():
            modulate(0, k, probe_ref[0, k], probe_ref[1, k])
        for s in range(1, slices):
            yield
            z = apply(0)
            yield
            for k in chunks():
                modulate(s, k, z[k, :width], z[k, width:])
        yield
        z = apply(2)
        yield
        for k in chunks():
            re, im = z[k, :width], z[k, width:]
            excess = re * re + im * im - pat_ref[slot, k].astype(f32)
            twice = excess + excess
            t_ref[k, :width] = (twice * re).astype(bf16)
            t_ref[k, width:] = (twice * im).astype(bf16)
        for s in range(slices - 1, -1, -1):
            yield
            g = apply_back(2 if s == slices - 1 else 0)
            yield
            for k in chunks():
                re, im = g[k], g[width + k.start : width + k.stop]
                grad = 0.5 * (im * phi_ref[s, 0, k] - re * phi_ref[s, 1, k])
                deposit(s, k, grad)
                if s:
                    cos, sin = cs_ref[s, 0, k], cs_ref[s, 1, k]
                    t_ref[k, :width] = (re * cos + im * sin).astype(bf16)
                    t_ref[k, width:] = (im * cos - re * sin).astype(bf16)

    def list_slot(slot, filled):
        order_ref[filled] = slot
        return filled + where_ref[slot, 2]

    filled = lax.fori_loop(0, slots, list_slot, 0)

    def pair(number, carry):
        first = one_window(order_ref[2 * number], *streams[:4])
        second = one_window(order_ref[2 * number + 1], *streams[4:])
        next(first)
        alive = True
        while alive:
            alive = False
            for stream in (first, second):
                alive = next(stream, True) is None or alive
        return carry

    lax.fori_loop(0, filled // 2, pair, 0)

    @pl.when(filled % 2 == 1)
    def _():
        for _ in one_window(order_ref[filled - 1], *streams[:4]):
            pass

    for s in range(slices):
        for b in range(blocks):
            part = acc_ref[s, every(0, tall, b)]
            if b < side:
                wout_ref[s, :, b * LANES : (b + 1) * LANES] = part.astype(bf16)
            elif b >= blocks - side:
                c = b - (blocks - side)
                eout_ref[s, :, c * LANES : (c + 1) * LANES] = part.astype(bf16)
            else:
                c = b - side
                mid_ref[s, :, c * LANES : (c + 1) * LANES] = part


def run_windows(where, own, up, down, west, east, probe, patterns, tables, interpret=False):
    slices, tile_y, tile_x = own.shape
    width = probe.shape[1]
    half = width // 2
    tall = tile_y + width
    f32, bf16 = jnp.float32, jnp.bfloat16
    vmem = pl.BlockSpec(memory_space=pltpu.VMEM)
    hbm = pl.BlockSpec(memory_space=pl.ANY)
    return pl.pallas_call(
        functools.partial(windows_kernel, half),
        out_shape=(
            jax.ShapeDtypeStruct((slices, tall, tile_x), f32),
            jax.ShapeDtypeStruct((slices, tall, half), bf16),
            jax.ShapeDtypeStruct((slices, tall, half), bf16),
        ),
        in_specs=[pl.BlockSpec(memory_space=pltpu.SMEM)] + [vmem] * 5 + [hbm, vmem, hbm],
        out_specs=(vmem,) * 3,
        scratch_shapes=[
            pltpu.VMEM((slices, tall * PITCH, LANES), f32),
            pltpu.VMEM((slices, tall * PITCH, LANES), f32),
            pltpu.SMEM((patterns.shape[0] + 1,), jnp.int32),
            pltpu.VMEM(probe.shape, f32),
            pltpu.VMEM(tables.shape, bf16),
            pltpu.SemaphoreType.DMA((2,)),
        ]
        + [
            pltpu.VMEM((slices, 2, width, width), f32),
            pltpu.VMEM((slices, 2, width, width), f32),
            pltpu.VMEM((2 * width, width), bf16),
            pltpu.VMEM((width, 2 * width), bf16),
        ]
        * 2,
        compiler_params=pltpu.CompilerParams(vmem_limit_bytes=40 << 20),
        interpret=interpret,
    )(where, own, up, down, west, east, probe, patterns, tables)


def pack_kernel(centers_ref, own_ref, pat_ref, sent_ref, rounded_ref):
    slots, _, width = sent_ref.shape
    tile_y, tile_x = own_ref.shape[1:]
    bf16 = jnp.bfloat16
    count = pat_ref.shape[0]
    lane = lax.broadcasted_iota(jnp.int32, (SLOT_PAD, width), 1)
    owners = [centers_ref[p, 1] // tile_x for p in range(count)]
    infos = []
    for p in range(count):
        row = centers_ref[p, 0] % tile_y
        col = centers_ref[p, 1] % tile_x
        info = jnp.where(lane == 0, row, jnp.where(lane == 1, col, jnp.where(lane == 2, 1, 0)))
        infos.append(info.astype(jnp.float32).astype(bf16))
    sent_ref[...] = jnp.zeros(sent_ref.shape, bf16)
    for p in range(count):
        sent_ref[owners[p], :width] = pat_ref[p]
        sent_ref[owners[p], width:] = infos[p]
    rounded_ref[...] = own_ref[...].astype(bf16)


def pack(centers, own, patterns, slots):
    width = patterns.shape[1]
    bf16 = jnp.bfloat16
    vmem = pl.BlockSpec(memory_space=pltpu.VMEM)
    return pl.pallas_call(
        pack_kernel,
        out_shape=(
            jax.ShapeDtypeStruct((slots, width + SLOT_PAD, width), bf16),
            jax.ShapeDtypeStruct(own.shape, bf16),
        ),
        in_specs=[pl.BlockSpec(memory_space=pltpu.SMEM), vmem, vmem],
        out_specs=(vmem,) * 2,
        compiler_params=pltpu.CompilerParams(vmem_limit_bytes=16 << 20),
    )(centers, own, patterns)


def shift(cells, axis, step):
    count = lax.axis_size(axis)
    pairs = [(i, i + step) for i in range(count) if 0 <= i + step < count]
    return lax.ppermute(cells, axis, pairs)


def per_device(tables, potential, probe, patterns, scan_centers):
    slices, tile_y, tile_x = potential.shape
    width = probe.shape[1]
    half = width // 2
    columns = lax.axis_size("tx")
    f32, bf16 = jnp.float32, jnp.bfloat16

    sent, rounded = pack(scan_centers, potential, patterns, columns)
    got = lax.all_to_all(sent, "tx", split_axis=0, concat_axis=0, tiled=True)
    where = got[:, width, :3].astype(f32).astype(jnp.int32)

    up = shift(rounded[:, tile_y - half :], "ty", 1)
    down = shift(rounded[:, :half], "ty", -1)

    def strip(cols):
        return jnp.concatenate([up[:, :, cols], rounded[:, :, cols], down[:, :, cols]], 1)

    west = shift(strip(slice(tile_x - half, tile_x)), "tx", 1)
    east = shift(strip(slice(0, half)), "tx", -1)

    mid, to_west, to_east = run_windows(
        where, potential, up, down, west, east, probe, got, tables
    )

    from_west = shift(to_east, "tx", 1)
    from_east = shift(to_west, "tx", -1)

    def with_sides(lo, hi):
        add = jnp.concatenate([from_west[:, lo:hi], from_east[:, lo:hi]], 2)
        return mid[:, lo:hi] + add.astype(f32)

    from_up = shift(with_sides(half + tile_y, 2 * half + tile_y).astype(bf16), "ty", 1)
    from_down = shift(with_sides(0, half).astype(bf16), "ty", -1)
    return with_sides(half, half + tile_y) + jnp.concatenate([from_up, from_down], 1).astype(f32)


def solution(mesh):
    in_specs = (P(None, "ty", "tx"), P(), P(("ty", "tx"), None, None), P(("ty", "tx"), None))
    out_specs = P(None, "ty", "tx")

    def run(potential, probe, patterns, scan_centers):
        tables = jnp.asarray(make_tables(probe.shape[1]))
        return jax.shard_map(
            functools.partial(per_device, tables),
            mesh=mesh, in_specs=in_specs, out_specs=out_specs, check_vma=False,
        )(potential, probe, patterns, scan_centers)

    return run
```

```python
import functools
import math

import jax
import jax.numpy as jnp
import numpy as np
from jax import lax
from jax.experimental import pallas as pl
from jax.experimental.pallas import tpu as pltpu
from jax.sharding import PartitionSpec as P

fresnel = 41.0
band_reach = 20.0
LANES = 128
PITCH = 5
ROWS = 64
FORWARD_VMEM = 56 << 20
BACKWARD_VMEM = 56 << 20


def sin_cos_coefs(limit):
    nodes = np.cos((np.arange(512) + 0.5) * np.pi / 512)
    u = 0.5 * (nodes + 1.0)
    v = np.sqrt(u) * limit
    t = 0.5 * v
    sinc = np.where(t == 0, 0.5, np.sin(t) / np.where(v == 0, 1.0, v))
    scale = limit * limit
    a = np.polynomial.polynomial.polyfit(u, sinc, 6) / scale ** np.arange(7)
    b = np.polynomial.polynomial.polyfit(u, np.cos(t), 7) / scale ** np.arange(8)
    return [float(np.float32(x)) for x in a], [float(np.float32(x)) for x in b]


SIN_COEFS, COS_COEFS = sin_cos_coefs(6.0)


def sin_cos_half(v):
    u = v * v
    s = SIN_COEFS[-1]
    for a in SIN_COEFS[-2::-1]:
        s = s * u + a
    c = COS_COEFS[-1]
    for b in COS_COEFS[-2::-1]:
        c = c * u + b
    return s * v, c


def make_tables(length):
    f32 = np.float32
    indices = np.arange(length, dtype=np.int32)
    gap = (indices[:, None] - indices[None, :]).astype(f32)
    chirp = f32(math.pi) * gap * gap / f32(fresnel)
    amplitude = (np.abs(gap) <= band_reach).astype(f32) / f32(math.sqrt(fresnel))
    product = indices[:, None] * indices[None, :] % length
    angle = f32(-2.0 * math.pi) * product.astype(f32) / f32(length)
    norm = f32(1.0 / math.sqrt(length))
    pairs = [
        (amplitude * np.cos(chirp), amplitude * np.sin(chirp)),
        (np.cos(angle) * norm, np.sin(angle) * norm),
    ]
    tables = []
    for re, im in pairs:
        left = np.block([[re, -im], [im, re]])
        right = np.block([[re, im], [-im, re]])
        tables += [left.astype(jnp.bfloat16), right.astype(jnp.bfloat16)]
    return np.stack(tables)


def dot(a, b):
    return jnp.dot(a, b, preferred_element_type=jnp.float32)


def every(start, count, block):
    return pl.ds(start * PITCH + block, count, stride=PITCH)


def spans(width):
    return [slice(k, k + ROWS) for k in range(0, width, ROWS)]


def place(where_ref, slot):
    row, col = where_ref[slot, 0], where_ref[slot, 1]
    block = col // LANES
    return row, block, col - block * LANES


def list_windows(where_ref, order_ref):
    slots = where_ref.shape[0]

    def body(slot, counts):
        filled, empty = counts
        full = where_ref[slot, 2] > 0
        order_ref[jnp.where(full, filled, slots - 1 - empty)] = slot
        return filled + jnp.where(full, 1, 0), empty + jnp.where(full, 0, 1)

    zero = jnp.zeros((), jnp.int32)
    filled, _ = lax.fori_loop(0, slots, body, (zero, zero))
    return (filled + 1) // 2


def alternate(first, second):
    next(first)
    alive = True
    while alive:
        alive = False
        for stream in (first, second):
            alive = next(stream, True) is None or alive


def forward_kernel(
    half, where_ref, own_hbm, up_ref, down_ref, west_ref, east_ref, probe_hbm, tab_hbm,
    phi_hbm, cs_hbm,
    ext_ref, order_ref, own_ref, probe_ref, tab_ref, sems, t_refs, phi_bufs, cs_bufs, out_sems,
):
    loads = [
        pltpu.make_async_copy(own_hbm, own_ref, sems.at[0]),
        pltpu.make_async_copy(tab_hbm.at[pl.ds(0, 2)], tab_ref, sems.at[1]),
        pltpu.make_async_copy(probe_hbm, probe_ref, sems.at[2]),
    ]
    for load in loads:
        load.start()
    slices, tile_y, tile_x = own_ref.shape
    width = probe_ref.shape[1]
    f32, bf16 = jnp.float32, jnp.bfloat16
    tall = tile_y + width
    blocks = (tile_x + width) // LANES
    side = half // LANES
    halves = width // LANES
    for s in range(slices):
        for c in range(side):
            lanes = slice(c * LANES, (c + 1) * LANES)
            ext_ref[s, every(0, tall, c)] = west_ref[s, :, lanes].astype(f32)
            ext_ref[s, every(0, tall, blocks - side + c)] = east_ref[s, :, lanes].astype(f32)
        for c in range(blocks - 2 * side):
            lanes = slice(c * LANES, (c + 1) * LANES)
            ext_ref[s, every(0, half, side + c)] = up_ref[s, :, lanes].astype(f32)
            ext_ref[s, every(half + tile_y, half, side + c)] = down_ref[s, :, lanes].astype(f32)
    loads[0].wait()
    for s in range(slices):
        for c in range(blocks - 2 * side):
            inner = own_ref[s, :, c * LANES : (c + 1) * LANES].astype(bf16).astype(f32)
            ext_ref[s, every(half, tile_y, side + c)] = inner
    for load in loads[1:]:
        load.wait()

    def stores(i, slot, bank):
        return [
            pltpu.make_async_copy(phi_bufs[i].at[bank], phi_hbm.at[slot], out_sems.at[i, bank, 0]),
            pltpu.make_async_copy(cs_bufs[i].at[bank], cs_hbm.at[slot], out_sems.at[i, bank, 1]),
        ]

    def one_window(slot, bank, t_ref, phi_ref, cs_ref):
        row, block, turn = place(where_ref, slot)
        back = jnp.where(turn == 0, 0, LANES - turn)
        low = lax.broadcasted_iota(jnp.int32, (ROWS, LANES), 1) < LANES - turn

        def modulate(s, k, re, im):
            parts = [
                pltpu.roll(ext_ref[s, every(row + k.start, ROWS, block + j)], back, 1)
                for j in range(halves + 1)
            ]
            for j in range(halves):
                c = slice(j * LANES, (j + 1) * LANES)
                sin, cos = sin_cos_half(jnp.where(low, parts[j], parts[j + 1]))
                if s:
                    cs_ref[bank, s - 1, 0, k, c] = cos
                    cs_ref[bank, s - 1, 1, k, c] = sin
                new_re = re[:, c] * cos - im[:, c] * sin
                new_im = re[:, c] * sin + im[:, c] * cos
                phi_ref[bank, s, k, c] = new_re.astype(bf16)
                phi_ref[bank, s, width + k.start : width + k.stop, c] = new_im.astype(bf16)

        for k in spans(width):
            modulate(0, k, probe_ref[0, k], probe_ref[1, k])
        for s in range(1, slices):
            yield
            mid = dot(tab_ref[0], phi_ref[bank, s - 1]).astype(bf16)
            t_ref[:, :width] = mid[:width]
            t_ref[:, width:] = mid[width:]
            z = dot(t_ref[...], tab_ref[1])
            yield
            for k in spans(width):
                modulate(s, k, z[k, :width], z[k, width:])

    pairs = list_windows(where_ref, order_ref)

    def settle(number):
        for i in range(2):
            for store in stores(i, order_ref[2 * number + i], lax.rem(number, 2)):
                store.wait()

    def pair(number, carry):
        bank = lax.rem(number, 2)

        @pl.when(number >= 2)
        def _():
            settle(number - 2)

        chosen = [order_ref[2 * number + i] for i in range(2)]
        alternate(
            *[one_window(chosen[i], bank, t_refs[i], phi_bufs[i], cs_bufs[i]) for i in range(2)]
        )
        for i in range(2):
            for store in stores(i, chosen[i], bank):
                store.start()
        return carry

    lax.fori_loop(0, pairs, pair, 0)
    lax.fori_loop(jnp.maximum(pairs - 2, 0), pairs, lambda n, c: (settle(n), c)[1], 0)


def backward_kernel(
    half, where_ref, phi_hbm, cs_hbm, pat_hbm, tab_hbm,
    mid_ref, wout_ref, eout_ref,
    acc_ref, order_ref, tab_ref, sem, s_refs, t_refs, phi_bufs, cs_bufs, pat_bufs, in_sems,
):
    table_load = pltpu.make_async_copy(tab_hbm, tab_ref, sem)
    table_load.start()
    slices = phi_hbm.shape[1]
    width = phi_hbm.shape[3]
    pairs = list_windows(where_ref, order_ref)

    def loads(number):
        bank = lax.rem(number, 2)
        found = []
        for i in range(2):
            slot = order_ref[2 * number + i]
            for j, (source, bufs) in enumerate(
                ((phi_hbm, phi_bufs), (cs_hbm, cs_bufs), (pat_hbm, pat_bufs))
            ):
                found.append(
                    pltpu.make_async_copy(source.at[slot], bufs[i].at[bank], in_sems.at[i, bank, j])
                )
        return found

    def fetch(number):
        @pl.when(number < pairs)
        def _():
            for load in loads(number):
                load.start()

    fetch(jnp.zeros((), jnp.int32))
    tall, tile_x = mid_ref.shape[1:]
    f32, bf16 = jnp.float32, jnp.bfloat16
    blocks = (tile_x + width) // LANES
    side = half // LANES
    halves = width // LANES
    for s in range(slices):
        acc_ref[s] = jnp.zeros(acc_ref.shape[1:], f32)
    table_load.wait()

    def one_window(slot, bank, s_ref, t_ref, phi_ref, cs_ref, pat_ref):
        row, block, turn = place(where_ref, slot)
        weight = jnp.where(where_ref[slot, 2] > 0, 0.5, 0.0)
        high = lax.broadcasted_iota(jnp.int32, (ROWS, LANES), 1) >= turn

        def deposit(s, k, grad):
            parts = [pltpu.roll(grad[:, j * LANES : (j + 1) * LANES], turn, 1) for j in range(halves)]
            zero = jnp.zeros((ROWS, LANES), f32)
            for j in range(halves + 1):
                here = parts[j] if j < halves else zero
                before = parts[j - 1] if j else zero
                acc_ref[s, every(row + k.start, ROWS, block + j)] += jnp.where(high, here, before)

        mid = dot(tab_ref[2], phi_ref[bank, slices - 1]).astype(bf16)
        t_ref[:, :width] = mid[:width]
        t_ref[:, width:] = mid[width:]
        z = dot(t_ref[...], tab_ref[3])
        yield
        for k in spans(width):
            re, im = z[k, :width], z[k, width:]
            excess = re * re + im * im - pat_ref[bank, k].astype(f32)
            twice = excess + excess
            t_ref[k, :width] = (twice * re).astype(bf16)
            t_ref[k, width:] = (twice * im).astype(bf16)
        for s in range(slices - 1, -1, -1):
            table = 2 if s == slices - 1 else 0
            yield
            mid = dot(t_ref[...], tab_ref[table]).astype(bf16)
            s_ref[:width] = mid[:, :width]
            s_ref[width:] = mid[:, width:]
            g = dot(tab_ref[table + 1], s_ref[...])
            yield
            for k in spans(width):
                below = slice(width + k.start, width + k.stop)
                re, im = g[k], g[below]
                phi_re, phi_im = phi_ref[bank, s, k].astype(f32), phi_ref[bank, s, below].astype(f32)
                deposit(s, k, weight * (im * phi_re - re * phi_im))
                if s:
                    cos, sin = cs_ref[bank, s - 1, 0, k], cs_ref[bank, s - 1, 1, k]
                    t_ref[k, :width] = (re * cos + im * sin).astype(bf16)
                    t_ref[k, width:] = (im * cos - re * sin).astype(bf16)

    def pair(number, carry):
        bank = lax.rem(number, 2)
        fetch(number + 1)
        for load in loads(number):
            load.wait()
        alternate(
            *[
                one_window(
                    order_ref[2 * number + i], bank, s_refs[i], t_refs[i],
                    phi_bufs[i], cs_bufs[i], pat_bufs[i],
                )
                for i in range(2)
            ]
        )
        return carry

    lax.fori_loop(0, pairs, pair, 0)
    for s in range(slices):
        for b in range(blocks):
            part = acc_ref[s, every(0, tall, b)]
            if b < side:
                wout_ref[s, :, b * LANES : (b + 1) * LANES] = part.astype(bf16)
            elif b >= blocks - side:
                c = b - (blocks - side)
                eout_ref[s, :, c * LANES : (c + 1) * LANES] = part.astype(bf16)
            else:
                c = b - side
                mid_ref[s, :, c * LANES : (c + 1) * LANES] = part


def run_forward(where, own, up, down, west, east, probe, tables, interpret=False):
    slices, tile_y, tile_x = own.shape
    width = probe.shape[1]
    slots = where.shape[0]
    f32, bf16 = jnp.float32, jnp.bfloat16
    vmem = pl.BlockSpec(memory_space=pltpu.VMEM)
    hbm = pl.BlockSpec(memory_space=pltpu.HBM)
    smem = pl.BlockSpec(memory_space=pltpu.SMEM)
    return pl.pallas_call(
        functools.partial(forward_kernel, width // 2),
        out_shape=(
            jax.ShapeDtypeStruct((slots, slices, 2 * width, width), bf16),
            jax.ShapeDtypeStruct((slots, slices - 1, 2, width, width), f32),
        ),
        in_specs=[smem, hbm] + [vmem] * 4 + [hbm] * 2,
        out_specs=(hbm,) * 2,
        scratch_shapes=[
            pltpu.VMEM((slices, (tile_y + width) * PITCH, LANES), f32),
            pltpu.SMEM((slots,), jnp.int32),
            pltpu.VMEM(own.shape, f32),
            pltpu.VMEM(probe.shape, f32),
            pltpu.VMEM((2,) + tables.shape[1:], bf16),
            pltpu.SemaphoreType.DMA((3,)),
            [pltpu.VMEM((width, 2 * width), bf16)] * 2,
            [pltpu.VMEM((2, slices, 2 * width, width), bf16)] * 2,
            [pltpu.VMEM((2, slices - 1, 2, width, width), f32)] * 2,
            pltpu.SemaphoreType.DMA((2, 2, 2)),
        ],
        compiler_params=pltpu.CompilerParams(vmem_limit_bytes=FORWARD_VMEM),
        interpret=interpret,
    )(where, own, up, down, west, east, probe, tables)


def run_backward(where, phi, cs, patterns, tables, tile_y, tile_x, interpret=False):
    slots, slices, _, width = phi.shape
    half = width // 2
    tall = tile_y + width
    f32, bf16 = jnp.float32, jnp.bfloat16
    vmem = pl.BlockSpec(memory_space=pltpu.VMEM)
    hbm = pl.BlockSpec(memory_space=pltpu.HBM)
    smem = pl.BlockSpec(memory_space=pltpu.SMEM)
    return pl.pallas_call(
        functools.partial(backward_kernel, half),
        out_shape=(
            jax.ShapeDtypeStruct((slices, tall, tile_x), f32),
            jax.ShapeDtypeStruct((slices, tall, half), bf16),
            jax.ShapeDtypeStruct((slices, tall, half), bf16),
        ),
        in_specs=[smem] + [hbm] * 4,
        out_specs=(vmem,) * 3,
        scratch_shapes=[
            pltpu.VMEM((slices, tall * PITCH, LANES), f32),
            pltpu.SMEM((slots,), jnp.int32),
            pltpu.VMEM(tables.shape, bf16),
            pltpu.SemaphoreType.DMA(()),
            [pltpu.VMEM((2 * width, width), bf16)] * 2,
            [pltpu.VMEM((width, 2 * width), bf16)] * 2,
            [pltpu.VMEM((2, slices, 2 * width, width), bf16)] * 2,
            [pltpu.VMEM((2, slices - 1, 2, width, width), f32)] * 2,
            [pltpu.VMEM((2, width, width), bf16)] * 2,
            pltpu.SemaphoreType.DMA((2, 2, 3)),
        ],
        compiler_params=pltpu.CompilerParams(vmem_limit_bytes=BACKWARD_VMEM),
        interpret=interpret,
    )(where, phi, cs, patterns, tables)


def pack_kernel(centers_ref, own_hbm, pat_hbm, sent_ref, info_ref, rounded_ref, own_ref, pat_ref, sems):
    loads = [
        pltpu.make_async_copy(own_hbm, own_ref, sems.at[0]),
        pltpu.make_async_copy(pat_hbm, pat_ref, sems.at[1]),
    ]
    for load in loads:
        load.start()
    tile_y, tile_x = own_ref.shape[1:]
    count = pat_ref.shape[0]
    owners = [centers_ref[p, 1] // tile_x for p in range(count)]
    lane = lax.broadcasted_iota(jnp.int32, info_ref.shape[1:], 1)
    info_ref[...] = jnp.zeros(info_ref.shape, jnp.int32)
    sent_ref[...] = jnp.zeros(sent_ref.shape, jnp.bfloat16)
    for p in range(count):
        row = centers_ref[p, 0] % tile_y
        col = centers_ref[p, 1] % tile_x
        info_ref[owners[p]] = jnp.where(
            lane == 0, row, jnp.where(lane == 1, col, jnp.where(lane == 2, 1, 0))
        )
    loads[0].wait()
    rounded_ref[...] = own_ref[...].astype(jnp.bfloat16)
    loads[1].wait()
    for p in range(count):
        sent_ref[owners[p]] = pat_ref[p]


def pack(centers, own, patterns, slots):
    width = patterns.shape[1]
    bf16 = jnp.bfloat16
    vmem = pl.BlockSpec(memory_space=pltpu.VMEM)
    hbm = pl.BlockSpec(memory_space=pltpu.HBM)
    return pl.pallas_call(
        pack_kernel,
        out_shape=(
            jax.ShapeDtypeStruct((slots, width, width), bf16),
            jax.ShapeDtypeStruct((slots, 8, LANES), jnp.int32),
            jax.ShapeDtypeStruct(own.shape, bf16),
        ),
        in_specs=[pl.BlockSpec(memory_space=pltpu.SMEM), hbm, hbm],
        out_specs=(vmem,) * 3,
        scratch_shapes=[
            pltpu.VMEM(own.shape, jnp.float32),
            pltpu.VMEM(patterns.shape, bf16),
            pltpu.SemaphoreType.DMA((2,)),
        ],
        compiler_params=pltpu.CompilerParams(vmem_limit_bytes=56 << 20),
    )(centers, own, patterns)


def shift(cells, axis, step):
    count = lax.axis_size(axis)
    pairs = [(i, i + step) for i in range(count) if 0 <= i + step < count]
    return lax.ppermute(cells, axis, pairs)


def per_device(tables, potential, probe, patterns, scan_centers):
    slices, tile_y, tile_x = potential.shape
    width = probe.shape[1]
    half = width // 2
    columns = lax.axis_size("tx")
    f32, bf16 = jnp.float32, jnp.bfloat16

    sent, info, rounded = pack(scan_centers, potential, patterns, columns)
    up = shift(rounded[:, tile_y - half :], "ty", 1)
    down = shift(rounded[:, :half], "ty", -1)
    where = lax.all_to_all(info, "tx", split_axis=0, concat_axis=0, tiled=True)[:, 0, :3]

    def strip(cols):
        return jnp.concatenate([up[:, :, cols], rounded[:, :, cols], down[:, :, cols]], 1)

    to_east, to_west = strip(slice(tile_x - half, tile_x)), strip(slice(0, half))
    sent, to_east, to_west = lax.optimization_barrier((sent, to_east, to_west))
    west = shift(to_east, "tx", 1)
    east = shift(to_west, "tx", -1)
    got = lax.all_to_all(sent, "tx", split_axis=0, concat_axis=0, tiled=True)

    phi, cs = run_forward(where, potential, up, down, west, east, probe, tables)
    mid, to_west, to_east = run_backward(where, phi, cs, got, tables, tile_y, tile_x)

    from_west = shift(to_east, "tx", 1)
    from_east = shift(to_west, "tx", -1)

    def with_sides(lo, hi):
        add = jnp.concatenate([from_west[:, lo:hi], from_east[:, lo:hi]], 2)
        return mid[:, lo:hi] + add.astype(f32)

    from_up = shift(with_sides(half + tile_y, 2 * half + tile_y).astype(bf16), "ty", 1)
    from_down = shift(with_sides(0, half).astype(bf16), "ty", -1)
    return with_sides(half, half + tile_y) + jnp.concatenate([from_up, from_down], 1).astype(f32)


def solution(mesh):
    in_specs = (P(None, "ty", "tx"), P(), P(("ty", "tx"), None, None), P(("ty", "tx"), None))
    out_specs = P(None, "ty", "tx")

    def run(potential, probe, patterns, scan_centers):
        tables = jnp.asarray(make_tables(probe.shape[1]))
        return jax.shard_map(
            functools.partial(per_device, tables),
            mesh=mesh, in_specs=in_specs, out_specs=out_specs, check_vma=False,
        )(potential, probe, patterns, scan_centers)

    return run
```

```python
import functools
import math

import jax
import jax.numpy as jnp
import numpy as np
from jax import lax
from jax.experimental import pallas as pl
from jax.experimental.pallas import tpu as pltpu
from jax.sharding import PartitionSpec as P

fresnel = 41.0
band_reach = 20.0
SLOT_PAD = 16
TILE = 256
LANES = 128
PITCH = 5


def sin_cos_coefs(limit):
    nodes = np.cos((np.arange(512) + 0.5) * np.pi / 512)
    u = 0.5 * (nodes + 1.0)
    v = np.sqrt(u) * limit
    t = 0.5 * v
    sinc = np.where(t == 0, 0.5, np.sin(t) / np.where(v == 0, 1.0, v))
    scale = limit * limit
    a = np.polynomial.polynomial.polyfit(u, sinc, 6) / scale ** np.arange(7)
    b = np.polynomial.polynomial.polyfit(u, np.cos(t), 7) / scale ** np.arange(8)
    return [float(np.float32(x)) for x in a], [float(np.float32(x)) for x in b]


SIN_COEFS, COS_COEFS = sin_cos_coefs(6.0)


def sin_cos_half(v):
    u = v * v
    s = SIN_COEFS[-1]
    for a in SIN_COEFS[-2::-1]:
        s = s * u + a
    c = COS_COEFS[-1]
    for b in COS_COEFS[-2::-1]:
        c = c * u + b
    return s * v, c


def make_tables(length):
    f32 = np.float32
    indices = np.arange(length, dtype=np.int32)
    gap = (indices[:, None] - indices[None, :]).astype(f32)
    chirp = f32(math.pi) * gap * gap / f32(fresnel)
    amplitude = (np.abs(gap) <= band_reach).astype(f32) / f32(math.sqrt(fresnel))
    product = indices[:, None] * indices[None, :] % length
    angle = f32(-2.0 * math.pi) * product.astype(f32) / f32(length)
    norm = f32(1.0 / math.sqrt(length))
    pairs = [
        (amplitude * np.cos(chirp), amplitude * np.sin(chirp)),
        (np.cos(angle) * norm, np.sin(angle) * norm),
    ]
    tables = []
    for re, im in pairs:
        left = np.block([[re, -im], [im, re]])
        right = np.block([[re, im], [-im, re]])
        tables += [left.astype(jnp.bfloat16), right.astype(jnp.bfloat16)]
    return np.stack(tables)


def windows_kernel(
    half, where_ref, own_hbm, up_ref, down_ref, west_ref, east_ref, probe_hbm, pat_hbm, tab_hbm,
    mid_ref, wout_ref, eout_ref,
    ext_ref, acc_ref, order_ref, own_ref, probe_ref, pat_ref, tab_ref, sems, *streams,
):
    loads = [
        pltpu.make_async_copy(own_hbm, own_ref, sems.at[0]),
        pltpu.make_async_copy(tab_hbm, tab_ref, sems.at[1]),
        pltpu.make_async_copy(probe_hbm, probe_ref, sems.at[2]),
        pltpu.make_async_copy(pat_hbm, pat_ref, sems.at[3]),
    ]
    for load in loads:
        load.start()
    slices, tile_y, tile_x = own_ref.shape
    width = probe_ref.shape[1]
    slots = pat_ref.shape[0]
    rows = 64
    f32, bf16 = jnp.float32, jnp.bfloat16
    tall = tile_y + width
    blocks = (tile_x + width) // LANES
    side = half // LANES
    halves = width // LANES

    def every(start, count, block):
        return pl.ds(start * PITCH + block, count, stride=PITCH)

    for s in range(slices):
        for c in range(side):
            lanes = slice(c * LANES, (c + 1) * LANES)
            ext_ref[s, every(0, tall, c)] = west_ref[s, :, lanes].astype(f32)
            ext_ref[s, every(0, tall, blocks - side + c)] = east_ref[s, :, lanes].astype(f32)
        for c in range(blocks - 2 * side):
            lanes = slice(c * LANES, (c + 1) * LANES)
            ext_ref[s, every(0, half, side + c)] = up_ref[s, :, lanes].astype(f32)
            ext_ref[s, every(half + tile_y, half, side + c)] = down_ref[s, :, lanes].astype(f32)
        acc_ref[s] = jnp.zeros(acc_ref.shape[1:], f32)
    loads[0].wait()
    for s in range(slices):
        for c in range(blocks - 2 * side):
            inner = own_ref[s, :, c * LANES : (c + 1) * LANES].astype(bf16).astype(f32)
            ext_ref[s, every(half, tile_y, side + c)] = inner
    for load in loads[1:]:
        load.wait()

    def dot(a, b):
        return jnp.dot(a, b, preferred_element_type=f32)

    def chunks():
        return [slice(k * rows, (k + 1) * rows) for k in range(width // rows)]

    def one_window(slot, cs_ref, phi_ref, s_ref, t_ref):
        row = where_ref[slot, 0]
        col = where_ref[slot, 1]
        block = col // LANES
        turn = col - block * LANES
        back = jnp.where(turn == 0, 0, LANES - turn)
        lane = lax.broadcasted_iota(jnp.int32, (rows, LANES), 1)
        low = lane < LANES - turn
        high = lane >= turn

        def modulate(s, k, re, im):
            parts = [
                pltpu.roll(ext_ref[s, every(row + k.start, rows, block + j)], back, 1)
                for j in range(halves + 1)
            ]
            for j in range(halves):
                c = slice(j * LANES, (j + 1) * LANES)
                sin, cos = sin_cos_half(jnp.where(low, parts[j], parts[j + 1]))
                cs_ref[s, 0, k, c] = cos
                cs_ref[s, 1, k, c] = sin
                new_re = re[:, c] * cos - im[:, c] * sin
                new_im = re[:, c] * sin + im[:, c] * cos
                phi_ref[s, 0, k, c] = new_re
                phi_ref[s, 1, k, c] = new_im
                s_ref[k, c] = new_re.astype(bf16)
                s_ref[width + k.start : width + k.stop, c] = new_im.astype(bf16)

        def deposit(s, k, grad):
            parts = [pltpu.roll(grad[:, j * LANES : (j + 1) * LANES], turn, 1) for j in range(halves)]
            zero = jnp.zeros((rows, LANES), f32)
            for j in range(halves + 1):
                here = parts[j] if j < halves else zero
                before = parts[j - 1] if j else zero
                acc_ref[s, every(row + k.start, rows, block + j)] += jnp.where(high, here, before)

        def apply(table):
            mid = dot(tab_ref[table], s_ref[...]).astype(bf16)
            t_ref[:, :width] = mid[:width]
            t_ref[:, width:] = mid[width:]
            return dot(t_ref[...], tab_ref[table + 1])

        def apply_back(table):
            mid = dot(t_ref[...], tab_ref[table]).astype(bf16)
            s_ref[:width] = mid[:, :width]
            s_ref[width:] = mid[:, width:]
            return dot(tab_ref[table + 1], s_ref[...])

        for k in chunks():
            modulate(0, k, probe_ref[0, k], probe_ref[1, k])
        for s in range(1, slices):
            yield
            z = apply(0)
            yield
            for k in chunks():
                modulate(s, k, z[k, :width], z[k, width:])
        yield
        z = apply(2)
        yield
        for k in chunks():
            re, im = z[k, :width], z[k, width:]
            excess = re * re + im * im - pat_ref[slot, k].astype(f32)
            twice = excess + excess
            t_ref[k, :width] = (twice * re).astype(bf16)
            t_ref[k, width:] = (twice * im).astype(bf16)
        for s in range(slices - 1, -1, -1):
            yield
            g = apply_back(2 if s == slices - 1 else 0)
            yield
            for k in chunks():
                re, im = g[k], g[width + k.start : width + k.stop]
                grad = 0.5 * (im * phi_ref[s, 0, k] - re * phi_ref[s, 1, k])
                deposit(s, k, grad)
                if s:
                    cos, sin = cs_ref[s, 0, k], cs_ref[s, 1, k]
                    t_ref[k, :width] = (re * cos + im * sin).astype(bf16)
                    t_ref[k, width:] = (im * cos - re * sin).astype(bf16)

    def list_slot(slot, filled):
        order_ref[filled] = slot
        return filled + where_ref[slot, 2]

    filled = lax.fori_loop(0, slots, list_slot, 0)

    def pair(number, carry):
        first = one_window(order_ref[2 * number], *streams[:4])
        second = one_window(order_ref[2 * number + 1], *streams[4:])
        next(first)
        alive = True
        while alive:
            alive = False
            for stream in (first, second):
                alive = next(stream, True) is None or alive
        return carry

    lax.fori_loop(0, filled // 2, pair, 0)

    @pl.when(filled % 2 == 1)
    def _():
        for _ in one_window(order_ref[filled - 1], *streams[:4]):
            pass

    for s in range(slices):
        for b in range(blocks):
            part = acc_ref[s, every(0, tall, b)]
            if b < side:
                wout_ref[s, :, b * LANES : (b + 1) * LANES] = part.astype(bf16)
            elif b >= blocks - side:
                c = b - (blocks - side)
                eout_ref[s, :, c * LANES : (c + 1) * LANES] = part.astype(bf16)
            else:
                c = b - side
                mid_ref[s, :, c * LANES : (c + 1) * LANES] = part


def run_windows(where, own, up, down, west, east, probe, patterns, tables, interpret=False):
    slices, tile_y, tile_x = own.shape
    width = probe.shape[1]
    half = width // 2
    tall = tile_y + width
    f32, bf16 = jnp.float32, jnp.bfloat16
    vmem = pl.BlockSpec(memory_space=pltpu.VMEM)
    hbm = pl.BlockSpec(memory_space=pltpu.HBM)
    return pl.pallas_call(
        functools.partial(windows_kernel, half),
        out_shape=(
            jax.ShapeDtypeStruct((slices, tall, tile_x), f32),
            jax.ShapeDtypeStruct((slices, tall, half), bf16),
            jax.ShapeDtypeStruct((slices, tall, half), bf16),
        ),
        in_specs=[pl.BlockSpec(memory_space=pltpu.SMEM), hbm] + [vmem] * 4 + [hbm] * 3,
        out_specs=(vmem,) * 3,
        scratch_shapes=[
            pltpu.VMEM((slices, tall * PITCH, LANES), f32),
            pltpu.VMEM((slices, tall * PITCH, LANES), f32),
            pltpu.SMEM((patterns.shape[0] + 1,), jnp.int32),
            pltpu.VMEM(own.shape, f32),
            pltpu.VMEM(probe.shape, f32),
            pltpu.VMEM(patterns.shape, bf16),
            pltpu.VMEM(tables.shape, bf16),
            pltpu.SemaphoreType.DMA((4,)),
        ]
        + [
            pltpu.VMEM((slices, 2, width, width), f32),
            pltpu.VMEM((slices, 2, width, width), f32),
            pltpu.VMEM((2 * width, width), bf16),
            pltpu.VMEM((width, 2 * width), bf16),
        ]
        * 2,
        compiler_params=pltpu.CompilerParams(vmem_limit_bytes=56 << 20),
        interpret=interpret,
    )(where, own, up, down, west, east, probe, patterns, tables)


def edges_kernel(own_ref, up_ref, down_ref, west_ref, east_ref):
    half = up_ref.shape[1]
    tile_y, tile_x = own_ref.shape[1:]
    bf16 = jnp.bfloat16
    up_ref[...] = own_ref[:, :half].astype(bf16)
    down_ref[...] = own_ref[:, tile_y - half :].astype(bf16)
    west_ref[...] = own_ref[:, :, :half].astype(bf16)
    east_ref[...] = own_ref[:, :, tile_x - half :].astype(bf16)


def edges(own, half):
    slices, tile_y, tile_x = own.shape
    bf16 = jnp.bfloat16
    flat = jax.ShapeDtypeStruct((slices, half, tile_x), bf16)
    tall = jax.ShapeDtypeStruct((slices, tile_y, half), bf16)

    def slab(shape):
        return pl.BlockSpec((1,) + shape[1:], lambda s: (s, 0, 0))

    return pl.pallas_call(
        edges_kernel,
        grid=(slices,),
        out_shape=(flat, flat, tall, tall),
        in_specs=[slab(own.shape)],
        out_specs=tuple(slab(x.shape) for x in (flat, flat, tall, tall)),
        compiler_params=pltpu.CompilerParams(vmem_limit_bytes=56 << 20),
    )(own)


def parcel_kernel(centers_ref, pat_ref, sent_ref):
    slots, _, width = sent_ref.shape
    bf16 = jnp.bfloat16
    lane = lax.broadcasted_iota(jnp.int32, (SLOT_PAD, width), 1)
    sent_ref[...] = jnp.zeros(sent_ref.shape, bf16)
    for p in range(pat_ref.shape[0]):
        owner = centers_ref[p, 1] // TILE
        row = centers_ref[p, 0] % TILE
        col = centers_ref[p, 1] % TILE
        info = jnp.where(lane == 0, row, jnp.where(lane == 1, col, jnp.where(lane == 2, 1, 0)))
        sent_ref[owner, :width] = pat_ref[p]
        sent_ref[owner, width:] = info.astype(jnp.float32).astype(bf16)


def parcels(centers, patterns, slots):
    width = patterns.shape[1]
    vmem = pl.BlockSpec(memory_space=pltpu.VMEM)
    return pl.pallas_call(
        parcel_kernel,
        out_shape=jax.ShapeDtypeStruct((slots, width + SLOT_PAD, width), jnp.bfloat16),
        in_specs=[pl.BlockSpec(memory_space=pltpu.SMEM), vmem],
        out_specs=vmem,
        compiler_params=pltpu.CompilerParams(vmem_limit_bytes=56 << 20),
    )(centers, patterns)


def shift(cells, axis, step):
    count = lax.axis_size(axis)
    pairs = [(i, i + step) for i in range(count) if 0 <= i + step < count]
    return lax.ppermute(cells, axis, pairs)


def per_device(tables, potential, probe, patterns, scan_centers):
    slices, tile_y, tile_x = potential.shape
    width = probe.shape[1]
    half = width // 2
    columns = lax.axis_size("tx")
    f32, bf16 = jnp.float32, jnp.bfloat16

    first_rows, last_rows, first_cols, last_cols = edges(potential, half)
    up = shift(last_rows, "ty", 1)
    down = shift(first_rows, "ty", -1)

    sent = parcels(scan_centers, patterns, columns)
    got = lax.all_to_all(sent, "tx", split_axis=0, concat_axis=0, tiled=True)
    where = got[:, width, :3].astype(f32).astype(jnp.int32)

    west = shift(
        jnp.concatenate([up[:, :, tile_x - half :], last_cols, down[:, :, tile_x - half :]], 1), "tx", 1
    )
    east = shift(jnp.concatenate([up[:, :, :half], first_cols, down[:, :, :half]], 1), "tx", -1)

    mid, to_west, to_east = run_windows(
        where, potential, up, down, west, east, probe, got, tables
    )

    from_west = shift(to_east, "tx", 1)
    from_east = shift(to_west, "tx", -1)

    def with_sides(lo, hi):
        add = jnp.concatenate([from_west[:, lo:hi], from_east[:, lo:hi]], 2)
        return mid[:, lo:hi] + add.astype(f32)

    from_up = shift(with_sides(half + tile_y, 2 * half + tile_y).astype(bf16), "ty", 1)
    from_down = shift(with_sides(0, half).astype(bf16), "ty", -1)
    return with_sides(half, half + tile_y) + jnp.concatenate([from_up, from_down], 1).astype(f32)


def solution(mesh):
    in_specs = (P(None, "ty", "tx"), P(), P(("ty", "tx"), None, None), P(("ty", "tx"), None))
    out_specs = P(None, "ty", "tx")

    def run(potential, probe, patterns, scan_centers):
        tables = jnp.asarray(make_tables(probe.shape[1]))
        return jax.shard_map(
            functools.partial(per_device, tables),
            mesh=mesh, in_specs=in_specs, out_specs=out_specs, check_vma=False,
        )(potential, probe, patterns, scan_centers)

    return run
```

```python
import functools
import math

import jax
import jax.numpy as jnp
import numpy as np
from jax import lax
from jax.experimental import pallas as pl
from jax.experimental.pallas import tpu as pltpu
from jax.sharding import PartitionSpec as P

fresnel = 41.0
band_reach = 20.0
SLOT_PAD = 16
TILE = 256
LANES = 128
PITCH = 5


def sin_cos_coefs(limit):
    nodes = np.cos((np.arange(512) + 0.5) * np.pi / 512)
    u = 0.5 * (nodes + 1.0)
    v = np.sqrt(u) * limit
    t = 0.25 * v
    scale = limit * limit
    a = np.polynomial.polynomial.polyfit(u, 2 * np.sin(t) / v, 5) / scale ** np.arange(6)
    b = np.polynomial.polynomial.polyfit(u, np.cos(t), 5) / scale ** np.arange(6)
    return [float(np.float32(x)) for x in a], [float(np.float32(x)) for x in b]


SIN_COEFS, COS_COEFS = sin_cos_coefs(6.0)


def sin_cos_half(v):
    u = v * v
    s = SIN_COEFS[-1]
    for a in SIN_COEFS[-2::-1]:
        s = s * u + a
    c = COS_COEFS[-1]
    for b in COS_COEFS[-2::-1]:
        c = c * u + b
    s = s * v
    return s * c, 1.0 - 0.5 * (s * s)


def make_tables(length):
    f32 = np.float32
    indices = np.arange(length, dtype=np.int32)
    gap = (indices[:, None] - indices[None, :]).astype(f32)
    chirp = f32(math.pi) * gap * gap / f32(fresnel)
    amplitude = (np.abs(gap) <= band_reach).astype(f32) / f32(math.sqrt(fresnel))
    product = indices[:, None] * indices[None, :] % length
    angle = f32(-2.0 * math.pi) * product.astype(f32) / f32(length)
    norm = f32(1.0 / math.sqrt(length))
    pairs = [
        (amplitude * np.cos(chirp), amplitude * np.sin(chirp)),
        (np.cos(angle) * norm, np.sin(angle) * norm),
    ]
    tables = []
    for re, im in pairs:
        left = np.block([[re, -im], [im, re]])
        right = np.block([[re, im], [-im, re]])
        tables += [left.astype(jnp.bfloat16), right.astype(jnp.bfloat16)]
    return np.stack(tables)


def windows_kernel(
    half, where_ref, own_hbm, up_hbm, down_hbm, west_hbm, east_hbm, probe_hbm, pat_hbm, tab_hbm,
    mid_hbm, wout_hbm, eout_hbm,
    ext_ref, acc_ref, order_ref, own_ref, up_ref, down_ref, west_ref, east_ref, probe_ref, pat_ref,
    tab_ref, mid_ref, wout_ref, eout_ref, in_sems, out_sems, *streams,
):
    sources = (west_hbm, east_hbm, up_hbm, down_hbm, own_hbm, tab_hbm, probe_hbm, pat_hbm)
    targets = (west_ref, east_ref, up_ref, down_ref, own_ref, tab_ref, probe_ref, pat_ref)
    loads = [
        pltpu.make_async_copy(source, into, in_sems.at[i])
        for i, (source, into) in enumerate(zip(sources, targets))
    ]
    for load in loads:
        load.start()
    slices, tile_y, tile_x = own_ref.shape
    width = probe_ref.shape[1]
    slots = pat_ref.shape[0]
    rows = 64
    f32, bf16 = jnp.float32, jnp.bfloat16
    tall = tile_y + width
    blocks = (tile_x + width) // LANES
    side = half // LANES
    halves = width // LANES

    def every(start, count, block):
        return pl.ds(start * PITCH + block, count, stride=PITCH)

    for s in range(slices):
        acc_ref[s] = jnp.zeros(acc_ref.shape[1:], f32)
    for load in loads[:2]:
        load.wait()
    for s in range(slices):
        for c in range(side):
            lanes = slice(c * LANES, (c + 1) * LANES)
            ext_ref[s, every(0, tall, c)] = west_ref[s, :, lanes].astype(f32)
            ext_ref[s, every(0, tall, blocks - side + c)] = east_ref[s, :, lanes].astype(f32)
    for load in loads[2:5]:
        load.wait()
    for s in range(slices):
        for c in range(blocks - 2 * side):
            lanes = slice(c * LANES, (c + 1) * LANES)
            ext_ref[s, every(0, half, side + c)] = up_ref[s, :, lanes].astype(f32)
            ext_ref[s, every(half + tile_y, half, side + c)] = down_ref[s, :, lanes].astype(f32)
            ext_ref[s, every(half, tile_y, side + c)] = own_ref[s, :, lanes].astype(bf16).astype(f32)
    for load in loads[5:]:
        load.wait()

    def dot(a, b):
        return jnp.dot(a, b, preferred_element_type=f32)

    def chunks():
        return [slice(k * rows, (k + 1) * rows) for k in range(width // rows)]

    def one_window(slot, cs_ref, phi_ref, s_ref, t_ref):
        row = where_ref[slot, 0]
        col = where_ref[slot, 1]
        block = col // LANES
        turn = col - block * LANES
        back = jnp.where(turn == 0, 0, LANES - turn)
        lane = lax.broadcasted_iota(jnp.int32, (rows, LANES), 1)
        low = lane < LANES - turn
        high = lane >= turn

        def modulate(s, k, re, im):
            parts = [
                pltpu.roll(ext_ref[s, every(row + k.start, rows, block + j)], back, 1)
                for j in range(halves + 1)
            ]
            for j in range(halves):
                c = slice(j * LANES, (j + 1) * LANES)
                sin, cos = sin_cos_half(jnp.where(low, parts[j], parts[j + 1]))
                cs_ref[s, 0, k, c] = cos
                cs_ref[s, 1, k, c] = sin
                new_re = re[:, c] * cos - im[:, c] * sin
                new_im = re[:, c] * sin + im[:, c] * cos
                phi_ref[s, 0, k, c] = new_re
                phi_ref[s, 1, k, c] = new_im
                s_ref[k, c] = new_re.astype(bf16)
                s_ref[width + k.start : width + k.stop, c] = new_im.astype(bf16)

        def deposit(s, k, grad):
            parts = [pltpu.roll(grad[:, j * LANES : (j + 1) * LANES], turn, 1) for j in range(halves)]
            zero = jnp.zeros((rows, LANES), f32)
            for j in range(halves + 1):
                here = parts[j] if j < halves else zero
                before = parts[j - 1] if j else zero
                acc_ref[s, every(row + k.start, rows, block + j)] += jnp.where(high, here, before)

        def apply(table):
            mid = dot(tab_ref[table], s_ref[...]).astype(bf16)
            t_ref[:, :width] = mid[:width]
            t_ref[:, width:] = mid[width:]
            return dot(t_ref[...], tab_ref[table + 1])

        def apply_back(table):
            mid = dot(t_ref[...], tab_ref[table]).astype(bf16)
            s_ref[:width] = mid[:, :width]
            s_ref[width:] = mid[:, width:]
            return dot(tab_ref[table + 1], s_ref[...])

        for k in chunks():
            modulate(0, k, probe_ref[0, k], probe_ref[1, k])
        for s in range(1, slices):
            yield
            z = apply(0)
            yield
            for k in chunks():
                modulate(s, k, z[k, :width], z[k, width:])
        yield
        z = apply(2)
        yield
        for k in chunks():
            re, im = z[k, :width], z[k, width:]
            excess = re * re + im * im - pat_ref[slot, k].astype(f32)
            twice = excess + excess
            t_ref[k, :width] = (twice * re).astype(bf16)
            t_ref[k, width:] = (twice * im).astype(bf16)
        for s in range(slices - 1, -1, -1):
            yield
            g = apply_back(2 if s == slices - 1 else 0)
            yield
            for k in chunks():
                re, im = g[k], g[width + k.start : width + k.stop]
                grad = 0.5 * (im * phi_ref[s, 0, k] - re * phi_ref[s, 1, k])
                deposit(s, k, grad)
                if s:
                    cos, sin = cs_ref[s, 0, k], cs_ref[s, 1, k]
                    t_ref[k, :width] = (re * cos + im * sin).astype(bf16)
                    t_ref[k, width:] = (im * cos - re * sin).astype(bf16)

    def list_slot(slot, filled):
        order_ref[filled] = slot
        return filled + where_ref[slot, 2]

    filled = lax.fori_loop(0, slots, list_slot, 0)

    def pair(number, carry):
        first = one_window(order_ref[2 * number], *streams[:4])
        second = one_window(order_ref[2 * number + 1], *streams[4:])
        next(first)
        alive = True
        while alive:
            alive = False
            for stream in (first, second):
                alive = next(stream, True) is None or alive
        return carry

    lax.fori_loop(0, filled // 2, pair, 0)

    @pl.when(filled % 2 == 1)
    def _():
        for _ in one_window(order_ref[filled - 1], *streams[:4]):
            pass

    stores = []
    for s in range(slices):
        for b in range(blocks):
            part = acc_ref[s, every(0, tall, b)]
            if b < side:
                wout_ref[s, :, b * LANES : (b + 1) * LANES] = part.astype(bf16)
            elif b >= blocks - side:
                c = b - (blocks - side)
                eout_ref[s, :, c * LANES : (c + 1) * LANES] = part.astype(bf16)
            else:
                c = b - side
                mid_ref[s, :, c * LANES : (c + 1) * LANES] = part
        for j, (source, into) in enumerate(
            ((mid_ref, mid_hbm), (wout_ref, wout_hbm), (eout_ref, eout_hbm))
        ):
            stores.append(pltpu.make_async_copy(source.at[s], into.at[s], out_sems.at[s, j]))
            stores[-1].start()
    for store in stores:
        store.wait()


def run_windows(where, own, up, down, west, east, probe, patterns, tables, interpret=False):
    slices, tile_y, tile_x = own.shape
    width = probe.shape[1]
    half = width // 2
    tall = tile_y + width
    f32, bf16 = jnp.float32, jnp.bfloat16
    hbm = pl.BlockSpec(memory_space=pltpu.HBM)
    return pl.pallas_call(
        functools.partial(windows_kernel, half),
        out_shape=(
            jax.ShapeDtypeStruct((slices, tall, tile_x), f32),
            jax.ShapeDtypeStruct((slices, tall, half), bf16),
            jax.ShapeDtypeStruct((slices, tall, half), bf16),
        ),
        in_specs=[pl.BlockSpec(memory_space=pltpu.SMEM)] + [hbm] * 8,
        out_specs=(hbm,) * 3,
        scratch_shapes=[
            pltpu.VMEM((slices, tall * PITCH, LANES), f32),
            pltpu.VMEM((slices, tall * PITCH, LANES), f32),
            pltpu.SMEM((patterns.shape[0] + 1,), jnp.int32),
        ]
        + [
            pltpu.VMEM(x.shape, x.dtype)
            for x in (own, up, down, west, east, probe, patterns, tables)
        ]
        + [
            pltpu.VMEM((slices, tall, tile_x), f32),
            pltpu.VMEM((slices, tall, half), bf16),
            pltpu.VMEM((slices, tall, half), bf16),
            pltpu.SemaphoreType.DMA((8,)),
            pltpu.SemaphoreType.DMA((slices, 3)),
        ]
        + [
            pltpu.VMEM((slices, 2, width, width), f32),
            pltpu.VMEM((slices, 2, width, width), f32),
            pltpu.VMEM((2 * width, width), bf16),
            pltpu.VMEM((width, 2 * width), bf16),
        ]
        * 2,
        compiler_params=pltpu.CompilerParams(vmem_limit_bytes=56 << 20),
        interpret=interpret,
    )(where, own, up, down, west, east, probe, patterns, tables)


def parcel_kernel(centers_ref, pat_hbm, sent_hbm, info_ref, sems):
    count, width, _ = pat_hbm.shape
    owners = [centers_ref[p, 1] // TILE for p in range(count)]
    copies = [
        pltpu.make_async_copy(pat_hbm.at[p], sent_hbm.at[owners[p], pl.ds(0, width)], sems.at[p])
        for p in range(count)
    ]
    for copy in copies:
        copy.start()
    lane = lax.broadcasted_iota(jnp.int32, info_ref.shape[1:], 1)
    info_ref[...] = jnp.zeros(info_ref.shape, jnp.bfloat16)
    for p in range(count):
        row = centers_ref[p, 0] % TILE
        col = centers_ref[p, 1] % TILE
        info = jnp.where(lane == 0, row, jnp.where(lane == 1, col, jnp.where(lane == 2, 1, 0)))
        info_ref[owners[p]] = info.astype(jnp.float32).astype(jnp.bfloat16)
    copies.append(
        pltpu.make_async_copy(info_ref, sent_hbm.at[:, pl.ds(width, SLOT_PAD)], sems.at[count])
    )
    copies[-1].start()
    for copy in copies:
        copy.wait()


def parcels(centers, patterns, slots):
    count, width, _ = patterns.shape
    hbm = pl.BlockSpec(memory_space=pltpu.HBM)
    return pl.pallas_call(
        parcel_kernel,
        out_shape=jax.ShapeDtypeStruct((slots, width + SLOT_PAD, width), jnp.bfloat16),
        in_specs=[pl.BlockSpec(memory_space=pltpu.SMEM), hbm],
        out_specs=hbm,
        scratch_shapes=[
            pltpu.VMEM((slots, SLOT_PAD, width), jnp.bfloat16),
            pltpu.SemaphoreType.DMA((count + 1,)),
        ],
        compiler_params=pltpu.CompilerParams(vmem_limit_bytes=56 << 20),
    )(centers, patterns)


def shift(cells, axis, step):
    count = lax.axis_size(axis)
    pairs = [(i, i + step) for i in range(count) if 0 <= i + step < count]
    return lax.ppermute(cells, axis, pairs)


def per_device(tables, potential, probe, patterns, scan_centers):
    slices, tile_y, tile_x = potential.shape
    width = probe.shape[1]
    half = width // 2
    columns = lax.axis_size("tx")
    f32, bf16 = jnp.float32, jnp.bfloat16

    rounded = potential.astype(bf16)
    up = shift(rounded[:, tile_y - half :], "ty", 1)
    down = shift(rounded[:, :half], "ty", -1)

    sent = parcels(scan_centers, patterns, columns)
    got = lax.all_to_all(sent, "tx", split_axis=0, concat_axis=0, tiled=True)
    where = got[:, width, :3].astype(f32).astype(jnp.int32)

    def strip(cols):
        return jnp.concatenate([up[:, :, cols], rounded[:, :, cols], down[:, :, cols]], 1)

    west = shift(strip(slice(tile_x - half, tile_x)), "tx", 1)
    east = shift(strip(slice(0, half)), "tx", -1)

    mid, to_west, to_east = run_windows(
        where, potential, up, down, west, east, probe, got, tables
    )

    from_west = shift(to_east, "tx", 1)
    from_east = shift(to_west, "tx", -1)

    def with_sides(lo, hi):
        add = jnp.concatenate([from_west[:, lo:hi], from_east[:, lo:hi]], 2)
        return mid[:, lo:hi] + add.astype(f32)

    from_up = shift(with_sides(half + tile_y, 2 * half + tile_y).astype(bf16), "ty", 1)
    from_down = shift(with_sides(0, half).astype(bf16), "ty", -1)
    return with_sides(half, half + tile_y) + jnp.concatenate([from_up, from_down], 1).astype(f32)


def solution(mesh):
    in_specs = (P(None, "ty", "tx"), P(), P(("ty", "tx"), None, None), P(("ty", "tx"), None))
    out_specs = P(None, "ty", "tx")

    def run(potential, probe, patterns, scan_centers):
        tables = jnp.asarray(make_tables(probe.shape[1]))
        return jax.shard_map(
            functools.partial(per_device, tables),
            mesh=mesh, in_specs=in_specs, out_specs=out_specs, check_vma=False,
        )(potential, probe, patterns, scan_centers)

    return run
```

```python
import functools
import math

import jax
import jax.numpy as jnp
import numpy as np
from jax import lax
from jax.experimental import pallas as pl
from jax.experimental.pallas import tpu as pltpu
from jax.sharding import PartitionSpec as P

fresnel = 41.0
band_reach = 20.0
SLOT_PAD = 16
TILE = 256
LANES = 128
PITCH = 5


def sin_cos_coefs(limit):
    nodes = np.cos((np.arange(512) + 0.5) * np.pi / 512)
    u = 0.5 * (nodes + 1.0)
    v = np.sqrt(u) * limit
    t = 0.25 * v
    scale = limit * limit
    a = np.polynomial.polynomial.polyfit(u, 2 * np.sin(t) / v, 5) / scale ** np.arange(6)
    b = np.polynomial.polynomial.polyfit(u, np.cos(t), 5) / scale ** np.arange(6)
    return [float(np.float32(x)) for x in a], [float(np.float32(x)) for x in b]


SIN_COEFS, COS_COEFS = sin_cos_coefs(6.0)


def sin_cos_half(v):
    u = v * v
    s = SIN_COEFS[-1]
    for a in SIN_COEFS[-2::-1]:
        s = s * u + a
    c = COS_COEFS[-1]
    for b in COS_COEFS[-2::-1]:
        c = c * u + b
    s = s * v
    return s * c, 1.0 - 0.5 * (s * s)


def make_tables(length):
    f32 = np.float32
    indices = np.arange(length, dtype=np.int32)
    gap = (indices[:, None] - indices[None, :]).astype(f32)
    chirp = f32(math.pi) * gap * gap / f32(fresnel)
    amplitude = (np.abs(gap) <= band_reach).astype(f32) / f32(math.sqrt(fresnel))
    product = indices[:, None] * indices[None, :] % length
    angle = f32(-2.0 * math.pi) * product.astype(f32) / f32(length)
    norm = f32(1.0 / math.sqrt(length))
    pairs = [
        (amplitude * np.cos(chirp), amplitude * np.sin(chirp)),
        (np.cos(angle) * norm, np.sin(angle) * norm),
    ]
    tables = []
    for re, im in pairs:
        left = np.block([[re, -im], [im, re]])
        right = np.block([[re, im], [-im, re]])
        tables += [left.astype(jnp.bfloat16), right.astype(jnp.bfloat16)]
    return np.stack(tables)


def windows_kernel(
    half, where_ref, own_hbm, up_hbm, down_hbm, west_hbm, east_hbm, probe_hbm, pat_hbm, tab_hbm,
    mid_hbm, wout_hbm, eout_hbm,
    ext_ref, acc_ref, order_ref, own_ref, up_ref, down_ref, west_ref, east_ref, probe_ref, pat_ref,
    tab_ref, mid_ref, wout_ref, eout_ref, in_sems, out_sems, *streams,
):
    sources = (west_hbm, east_hbm, up_hbm, down_hbm, own_hbm, tab_hbm, probe_hbm, pat_hbm)
    targets = (west_ref, east_ref, up_ref, down_ref, own_ref, tab_ref, probe_ref, pat_ref)
    loads = [
        pltpu.make_async_copy(source, into, in_sems.at[i])
        for i, (source, into) in enumerate(zip(sources, targets))
    ]
    for load in loads:
        load.start()
    slices, tile_y, tile_x = own_ref.shape
    width = probe_ref.shape[1]
    slots = pat_ref.shape[0]
    rows = 64
    f32, bf16 = jnp.float32, jnp.bfloat16
    tall = tile_y + width
    blocks = (tile_x + width) // LANES
    side = half // LANES
    halves = width // LANES

    def every(start, count, block):
        return pl.ds(start * PITCH + block, count, stride=PITCH)

    for s in range(slices):
        acc_ref[s] = jnp.zeros(acc_ref.shape[1:], f32)
    for load in loads[:2]:
        load.wait()
    for s in range(slices):
        for c in range(side):
            lanes = slice(c * LANES, (c + 1) * LANES)
            ext_ref[s, every(0, tall, c)] = west_ref[s, :, lanes].astype(f32)
            ext_ref[s, every(0, tall, blocks - side + c)] = east_ref[s, :, lanes].astype(f32)
    for load in loads[2:5]:
        load.wait()
    for s in range(slices):
        for c in range(blocks - 2 * side):
            lanes = slice(c * LANES, (c + 1) * LANES)
            ext_ref[s, every(0, half, side + c)] = up_ref[s, :, lanes].astype(f32)
            ext_ref[s, every(half + tile_y, half, side + c)] = down_ref[s, :, lanes].astype(f32)
            ext_ref[s, every(half, tile_y, side + c)] = own_ref[s, :, lanes].astype(bf16).astype(f32)
    for load in loads[5:]:
        load.wait()

    def dot(a, b):
        return jnp.dot(a, b, preferred_element_type=f32)

    def chunks():
        return [slice(k * rows, (k + 1) * rows) for k in range(width // rows)]

    def one_window(slot, cs_ref, phi_ref, s_ref, t_ref):
        row = where_ref[slot, 0]
        col = where_ref[slot, 1]
        block = col // LANES
        turn = col - block * LANES
        back = jnp.where(turn == 0, 0, LANES - turn)
        lane = lax.broadcasted_iota(jnp.int32, (rows, LANES), 1)
        low = lane < LANES - turn
        high = lane >= turn

        def modulate(s, k, re, im):
            parts = [
                pltpu.roll(ext_ref[s, every(row + k.start, rows, block + j)], back, 1)
                for j in range(halves + 1)
            ]
            for j in range(halves):
                c = slice(j * LANES, (j + 1) * LANES)
                sin, cos = sin_cos_half(jnp.where(low, parts[j], parts[j + 1]))
                cs_ref[s, 0, k, c] = cos
                cs_ref[s, 1, k, c] = sin
                new_re = re[:, c] * cos - im[:, c] * sin
                new_im = re[:, c] * sin + im[:, c] * cos
                phi_ref[s, 0, k, c] = new_re
                phi_ref[s, 1, k, c] = new_im
                s_ref[k, c] = new_re.astype(bf16)
                s_ref[width + k.start : width + k.stop, c] = new_im.astype(bf16)

        def deposit(s, k, grad):
            parts = [pltpu.roll(grad[:, j * LANES : (j + 1) * LANES], turn, 1) for j in range(halves)]
            zero = jnp.zeros((rows, LANES), f32)
            for j in range(halves + 1):
                here = parts[j] if j < halves else zero
                before = parts[j - 1] if j else zero
                acc_ref[s, every(row + k.start, rows, block + j)] += jnp.where(high, here, before)

        def apply(table):
            mid = dot(tab_ref[table], s_ref[...]).astype(bf16)
            t_ref[:, :width] = mid[:width]
            t_ref[:, width:] = mid[width:]
            return dot(t_ref[...], tab_ref[table + 1])

        def apply_back(table):
            mid = dot(t_ref[...], tab_ref[table]).astype(bf16)
            s_ref[:width] = mid[:, :width]
            s_ref[width:] = mid[:, width:]
            return dot(tab_ref[table + 1], s_ref[...])

        for k in chunks():
            modulate(0, k, probe_ref[0, k], probe_ref[1, k])
        for s in range(1, slices):
            yield
            z = apply(0)
            yield
            for k in chunks():
                modulate(s, k, z[k, :width], z[k, width:])
        yield
        z = apply(2)
        yield
        for k in chunks():
            re, im = z[k, :width], z[k, width:]
            excess = re * re + im * im - pat_ref[slot, k].astype(f32)
            t_ref[k, :width] = (excess * re).astype(bf16)
            t_ref[k, width:] = (excess * im).astype(bf16)
        for s in range(slices - 1, -1, -1):
            yield
            g = apply_back(2 if s == slices - 1 else 0)
            yield
            for k in chunks():
                re, im = g[k], g[width + k.start : width + k.stop]
                grad = im * phi_ref[s, 0, k] - re * phi_ref[s, 1, k]
                deposit(s, k, grad)
                if s:
                    cos, sin = cs_ref[s, 0, k], cs_ref[s, 1, k]
                    t_ref[k, :width] = (re * cos + im * sin).astype(bf16)
                    t_ref[k, width:] = (im * cos - re * sin).astype(bf16)

    def list_slot(slot, filled):
        order_ref[filled] = slot
        return filled + where_ref[slot, 2]

    filled = lax.fori_loop(0, slots, list_slot, 0)

    def pair(number, carry):
        first = one_window(order_ref[2 * number], *streams[:4])
        second = one_window(order_ref[2 * number + 1], *streams[4:])
        next(first)
        alive = True
        while alive:
            alive = False
            for stream in (first, second):
                alive = next(stream, True) is None or alive
        return carry

    lax.fori_loop(0, filled // 2, pair, 0)

    @pl.when(filled % 2 == 1)
    def _():
        for _ in one_window(order_ref[filled - 1], *streams[:4]):
            pass

    stores = []
    for s in range(slices):
        for b in range(blocks):
            part = acc_ref[s, every(0, tall, b)]
            if b < side:
                wout_ref[s, :, b * LANES : (b + 1) * LANES] = part.astype(bf16)
            elif b >= blocks - side:
                c = b - (blocks - side)
                eout_ref[s, :, c * LANES : (c + 1) * LANES] = part.astype(bf16)
            else:
                c = b - side
                mid_ref[s, :, c * LANES : (c + 1) * LANES] = part
        for j, (source, into) in enumerate(
            ((mid_ref, mid_hbm), (wout_ref, wout_hbm), (eout_ref, eout_hbm))
        ):
            stores.append(pltpu.make_async_copy(source.at[s], into.at[s], out_sems.at[s, j]))
            stores[-1].start()
    for store in stores:
        store.wait()


def run_windows(where, own, up, down, west, east, probe, patterns, tables, interpret=False):
    slices, tile_y, tile_x = own.shape
    width = probe.shape[1]
    half = width // 2
    tall = tile_y + width
    f32, bf16 = jnp.float32, jnp.bfloat16
    hbm = pl.BlockSpec(memory_space=pltpu.HBM)
    return pl.pallas_call(
        functools.partial(windows_kernel, half),
        out_shape=(
            jax.ShapeDtypeStruct((slices, tall, tile_x), f32),
            jax.ShapeDtypeStruct((slices, tall, half), bf16),
            jax.ShapeDtypeStruct((slices, tall, half), bf16),
        ),
        in_specs=[pl.BlockSpec(memory_space=pltpu.SMEM)] + [hbm] * 8,
        out_specs=(hbm,) * 3,
        scratch_shapes=[
            pltpu.VMEM((slices, tall * PITCH, LANES), f32),
            pltpu.VMEM((slices, tall * PITCH, LANES), f32),
            pltpu.SMEM((patterns.shape[0] + 1,), jnp.int32),
        ]
        + [
            pltpu.VMEM(x.shape, x.dtype)
            for x in (own, up, down, west, east, probe, patterns, tables)
        ]
        + [
            pltpu.VMEM((slices, tall, tile_x), f32),
            pltpu.VMEM((slices, tall, half), bf16),
            pltpu.VMEM((slices, tall, half), bf16),
            pltpu.SemaphoreType.DMA((8,)),
            pltpu.SemaphoreType.DMA((slices, 3)),
        ]
        + [
            pltpu.VMEM((slices, 2, width, width), f32),
            pltpu.VMEM((slices, 2, width, width), f32),
            pltpu.VMEM((2 * width, width), bf16),
            pltpu.VMEM((width, 2 * width), bf16),
        ]
        * 2,
        compiler_params=pltpu.CompilerParams(vmem_limit_bytes=56 << 20),
        interpret=interpret,
    )(where, own, up, down, west, east, probe, patterns, tables)


def parcel_kernel(centers_ref, pat_ref, sent_ref):
    slots, _, width = sent_ref.shape
    bf16 = jnp.bfloat16
    lane = lax.broadcasted_iota(jnp.int32, (SLOT_PAD, width), 1)
    sent_ref[...] = jnp.zeros(sent_ref.shape, bf16)
    for p in range(pat_ref.shape[0]):
        owner = centers_ref[p, 1] // TILE
        row = centers_ref[p, 0] % TILE
        col = centers_ref[p, 1] % TILE
        info = jnp.where(lane == 0, row, jnp.where(lane == 1, col, jnp.where(lane == 2, 1, 0)))
        sent_ref[owner, :width] = pat_ref[p]
        sent_ref[owner, width:] = info.astype(jnp.float32).astype(bf16)


def parcels(centers, patterns, slots):
    width = patterns.shape[1]
    vmem = pl.BlockSpec(memory_space=pltpu.VMEM)
    return pl.pallas_call(
        parcel_kernel,
        out_shape=jax.ShapeDtypeStruct((slots, width + SLOT_PAD, width), jnp.bfloat16),
        in_specs=[pl.BlockSpec(memory_space=pltpu.SMEM), vmem],
        out_specs=vmem,
        compiler_params=pltpu.CompilerParams(vmem_limit_bytes=56 << 20),
    )(centers, patterns)


def shift(cells, axis, step):
    count = lax.axis_size(axis)
    pairs = [(i, i + step) for i in range(count) if 0 <= i + step < count]
    return lax.ppermute(cells, axis, pairs)


def per_device(tables, potential, probe, patterns, scan_centers):
    slices, tile_y, tile_x = potential.shape
    width = probe.shape[1]
    half = width // 2
    columns = lax.axis_size("tx")
    f32, bf16 = jnp.float32, jnp.bfloat16

    rounded = potential.astype(bf16)
    up = shift(rounded[:, tile_y - half :], "ty", 1)
    down = shift(rounded[:, :half], "ty", -1)

    sent = parcels(scan_centers, patterns, columns)
    got = lax.all_to_all(sent, "tx", split_axis=0, concat_axis=0, tiled=True)
    where = got[:, width, :3].astype(f32).astype(jnp.int32)

    def strip(cols):
        return jnp.concatenate([up[:, :, cols], rounded[:, :, cols], down[:, :, cols]], 1)

    west = shift(strip(slice(tile_x - half, tile_x)), "tx", 1)
    east = shift(strip(slice(0, half)), "tx", -1)

    mid, to_west, to_east = run_windows(
        where, potential, up, down, west, east, probe, got, tables
    )

    from_west = shift(to_east, "tx", 1)
    from_east = shift(to_west, "tx", -1)

    def with_sides(lo, hi):
        add = jnp.concatenate([from_west[:, lo:hi], from_east[:, lo:hi]], 2)
        return mid[:, lo:hi] + add.astype(f32)

    from_up = shift(with_sides(half + tile_y, 2 * half + tile_y).astype(bf16), "ty", 1)
    from_down = shift(with_sides(0, half).astype(bf16), "ty", -1)
    return with_sides(half, half + tile_y) + jnp.concatenate([from_up, from_down], 1).astype(f32)


def solution(mesh):
    in_specs = (P(None, "ty", "tx"), P(), P(("ty", "tx"), None, None), P(("ty", "tx"), None))
    out_specs = P(None, "ty", "tx")

    def run(potential, probe, patterns, scan_centers):
        tables = jnp.asarray(make_tables(probe.shape[1]))
        return jax.shard_map(
            functools.partial(per_device, tables),
            mesh=mesh, in_specs=in_specs, out_specs=out_specs, check_vma=False,
        )(potential, probe, patterns, scan_centers)

    return run
```

```python
import functools
import math

import jax
import jax.numpy as jnp
import numpy as np
from jax import lax
from jax.experimental import pallas as pl
from jax.experimental.pallas import tpu as pltpu
from jax.sharding import PartitionSpec as P

fresnel = 41.0
band_reach = 20.0
SLOT_PAD = 16
TILE = 256
LANES = 128
PITCH = 5
GROUP = 2
STREAMS = 2


def sin_cos_coefs(limit):
    nodes = np.cos((np.arange(512) + 0.5) * np.pi / 512)
    u = 0.5 * (nodes + 1.0)
    v = np.sqrt(u) * limit
    t = 0.25 * v
    scale = limit * limit
    a = np.polynomial.polynomial.polyfit(u, 2 * np.sin(t) / v, 4) / scale ** np.arange(5)
    b = np.polynomial.polynomial.polyfit(u, np.cos(t), 4) / scale ** np.arange(5)
    return [float(np.float32(x)) for x in a], [float(np.float32(x)) for x in b]


SIN_COEFS, COS_COEFS = sin_cos_coefs(6.0)


def sin_cos_half(v):
    u = v * v
    s = SIN_COEFS[-1]
    for a in SIN_COEFS[-2::-1]:
        s = s * u + a
    c = COS_COEFS[-1]
    for b in COS_COEFS[-2::-1]:
        c = c * u + b
    s = s * v
    return s * c, 1.0 - 0.5 * (s * s)


def make_tables(length):
    f32 = np.float32
    indices = np.arange(length, dtype=np.int32)
    gap = (indices[:, None] - indices[None, :]).astype(f32)
    chirp = f32(math.pi) * gap * gap / f32(fresnel)
    amplitude = (np.abs(gap) <= band_reach).astype(f32) / f32(math.sqrt(fresnel))
    product = indices[:, None] * indices[None, :] % length
    angle = f32(-2.0 * math.pi) * product.astype(f32) / f32(length)
    norm = f32(1.0 / math.sqrt(length))
    pairs = [
        (amplitude * np.cos(chirp), amplitude * np.sin(chirp)),
        (np.cos(angle) * norm, np.sin(angle) * norm),
    ]
    tables = []
    for re, im in pairs:
        left = np.block([[re, -im], [im, re]])
        right = np.block([[re, im], [-im, re]])
        tables += [left.astype(jnp.bfloat16), right.astype(jnp.bfloat16)]
    return np.stack(tables)


def windows_kernel(
    half, where_ref, own_hbm, up_hbm, down_hbm, west_hbm, east_hbm, probe_hbm, pat_hbm, tab_hbm,
    mid_hbm, wout_hbm, eout_hbm,
    ext_ref, acc_ref, order_ref, own_ref, up_ref, down_ref, west_ref, east_ref, probe_ref, pat_ref,
    tab_ref, mid_ref, wout_ref, eout_ref, in_sems, out_sems, *streams,
):
    sources = (west_hbm, east_hbm, up_hbm, down_hbm, own_hbm, tab_hbm, probe_hbm, pat_hbm)
    targets = (west_ref, east_ref, up_ref, down_ref, own_ref, tab_ref, probe_ref, pat_ref)
    loads = [
        pltpu.make_async_copy(source, into, in_sems.at[i])
        for i, (source, into) in enumerate(zip(sources, targets))
    ]
    for load in loads:
        load.start()
    slices, tile_y, tile_x = own_ref.shape
    width = probe_ref.shape[1]
    slots = pat_ref.shape[0]
    rows = 64
    f32, bf16 = jnp.float32, jnp.bfloat16
    tall = tile_y + width
    blocks = (tile_x + width) // LANES
    side = half // LANES
    halves = width // LANES

    def every(start, count, block):
        return pl.ds(start * PITCH + block, count, stride=PITCH)

    for s in range(slices):
        acc_ref[s] = jnp.zeros(acc_ref.shape[1:], f32)
    for load in loads[:2]:
        load.wait()
    for s in range(slices):
        for c in range(side):
            lanes = slice(c * LANES, (c + 1) * LANES)
            ext_ref[s, every(0, tall, c)] = west_ref[s, :, lanes].astype(f32)
            ext_ref[s, every(0, tall, blocks - side + c)] = east_ref[s, :, lanes].astype(f32)
    for load in loads[2:5]:
        load.wait()
    for s in range(slices):
        for c in range(blocks - 2 * side):
            lanes = slice(c * LANES, (c + 1) * LANES)
            ext_ref[s, every(0, half, side + c)] = up_ref[s, :, lanes].astype(f32)
            ext_ref[s, every(half + tile_y, half, side + c)] = down_ref[s, :, lanes].astype(f32)
            ext_ref[s, every(half, tile_y, side + c)] = own_ref[s, :, lanes].astype(bf16).astype(f32)
    for load in loads[5:]:
        load.wait()

    def dot(a, b):
        return jnp.dot(a, b, preferred_element_type=f32)

    def chunks():
        return [slice(k * rows, (k + 1) * rows) for k in range(width // rows)]

    def group(slot_list, cs_ref, phi_ref, s_ref, t_ref):
        places = []
        lane = lax.broadcasted_iota(jnp.int32, (rows, LANES), 1)
        for slot in slot_list:
            row = where_ref[slot, 0]
            col = where_ref[slot, 1]
            block = col // LANES
            turn = col - block * LANES
            back = jnp.where(turn == 0, 0, LANES - turn)
            weight = jnp.where(where_ref[slot, 2] > 0, 1.0, 0.0)
            places.append((row, block, turn, back, lane < LANES - turn, lane >= turn, weight))

        def modulate(w, s, k, re, im):
            row, block, turn, back, low, high, weight = places[w]
            parts = [
                pltpu.roll(ext_ref[s, every(row + k.start, rows, block + j)], back, 1)
                for j in range(halves + 1)
            ]
            for j in range(halves):
                c = slice(j * LANES, (j + 1) * LANES)
                into = slice(w * width + c.start, w * width + c.stop)
                sin, cos = sin_cos_half(jnp.where(low, parts[j], parts[j + 1]))
                new_re = re[:, c] * cos - im[:, c] * sin
                new_im = re[:, c] * sin + im[:, c] * cos
                if s:
                    cs_ref[w, s, 0, k, c] = cos
                    cs_ref[w, s, 1, k, c] = sin
                phi_ref[w, s, 0, k, c] = new_re
                phi_ref[w, s, 1, k, c] = new_im
                s_ref[k, into] = new_re.astype(bf16)
                s_ref[width + k.start : width + k.stop, into] = new_im.astype(bf16)

        def deposit(w, s, k, grad):
            row, block, turn, back, low, high, weight = places[w]
            parts = [pltpu.roll(grad[:, j * LANES : (j + 1) * LANES], turn, 1) for j in range(halves)]
            zero = jnp.zeros((rows, LANES), f32)
            for j in range(halves + 1):
                here = parts[j] if j < halves else zero
                before = parts[j - 1] if j else zero
                acc_ref[s, every(row + k.start, rows, block + j)] += jnp.where(high, here, before)

        def span(w):
            return slice(w * width, (w + 1) * width)

        def left(table):
            return dot(tab_ref[table], s_ref[...])

        def right(table):
            return dot(t_ref[...], tab_ref[table])

        many = range(len(slot_list))
        for w in many:
            for k in chunks():
                modulate(w, 0, k, probe_ref[0, k], probe_ref[1, k])
        for s in range(1, slices + 1):
            table = 2 if s == slices else 0
            yield
            mid = left(table).astype(bf16)
            for w in many:
                t_ref[span(w), :width] = mid[:width, span(w)]
                t_ref[span(w), width:] = mid[width:, span(w)]
            z = right(table + 1)
            yield
            for w in many:
                for k in chunks():
                    own = slice(w * width + k.start, w * width + k.stop)
                    re, im = z[own, :width], z[own, width:]
                    if s < slices:
                        modulate(w, s, k, re, im)
                    else:
                        excess = re * re + im * im - pat_ref[slot_list[w], k].astype(f32)
                        t_ref[own, :width] = (excess * re).astype(bf16)
                        t_ref[own, width:] = (excess * im).astype(bf16)
        for s in range(slices - 1, -1, -1):
            table = 2 if s == slices - 1 else 0
            yield
            mid = right(table).astype(bf16)
            for w in many:
                s_ref[:width, span(w)] = mid[span(w), :width]
                s_ref[width:, span(w)] = mid[span(w), width:]
            g = left(table + 1)
            yield
            for w in many:
                for k in chunks():
                    own = slice(w * width + k.start, w * width + k.stop)
                    re, im = g[k, span(w)], g[width + k.start : width + k.stop, span(w)]
                    grad = places[w][-1] * (im * phi_ref[w, s, 0, k] - re * phi_ref[w, s, 1, k])
                    deposit(w, s, k, grad)
                    if s:
                        cos, sin = cs_ref[w, s, 0, k], cs_ref[w, s, 1, k]
                        t_ref[own, :width] = (re * cos + im * sin).astype(bf16)
                        t_ref[own, width:] = (im * cos - re * sin).astype(bf16)

    def list_slots(wanted):
        def body(slot, count):
            filled = where_ref[slot, 2] > 0

            @pl.when(filled == wanted)
            def _():
                order_ref[count] = slot

            return count + jnp.where(filled == wanted, 1, 0)

        return body

    filled = lax.fori_loop(0, slots, list_slots(True), 0)
    lax.fori_loop(0, slots, list_slots(False), filled)
    batch = STREAMS * GROUP

    def many_windows(number, carry):
        running = []
        for i in range(STREAMS):
            base = number * batch + i * GROUP
            chosen = [order_ref[base + w] for w in range(GROUP)]
            running.append(group(chosen, *streams[4 * i : 4 * i + 4]))
        for i, stream in enumerate(running):
            for _ in range(STREAMS - 1 - i):
                next(stream)
        alive = True
        while alive:
            alive = False
            for stream in running:
                alive = next(stream, True) is None or alive
        return carry

    lax.fori_loop(0, (filled + batch - 1) // batch, many_windows, 0)

    stores = []
    for s in range(slices):
        for b in range(blocks):
            part = acc_ref[s, every(0, tall, b)]
            if b < side:
                wout_ref[s, :, b * LANES : (b + 1) * LANES] = part.astype(bf16)
            elif b >= blocks - side:
                c = b - (blocks - side)
                eout_ref[s, :, c * LANES : (c + 1) * LANES] = part.astype(bf16)
            else:
                c = b - side
                mid_ref[s, :, c * LANES : (c + 1) * LANES] = part
        for j, (source, into) in enumerate(
            ((mid_ref, mid_hbm), (wout_ref, wout_hbm), (eout_ref, eout_hbm))
        ):
            stores.append(pltpu.make_async_copy(source.at[s], into.at[s], out_sems.at[s, j]))
            stores[-1].start()
    for store in stores:
        store.wait()


def run_windows(where, own, up, down, west, east, probe, patterns, tables, interpret=False):
    slices, tile_y, tile_x = own.shape
    width = probe.shape[1]
    half = width // 2
    tall = tile_y + width
    f32, bf16 = jnp.float32, jnp.bfloat16
    hbm = pl.BlockSpec(memory_space=pltpu.HBM)
    return pl.pallas_call(
        functools.partial(windows_kernel, half),
        out_shape=(
            jax.ShapeDtypeStruct((slices, tall, tile_x), f32),
            jax.ShapeDtypeStruct((slices, tall, half), bf16),
            jax.ShapeDtypeStruct((slices, tall, half), bf16),
        ),
        in_specs=[pl.BlockSpec(memory_space=pltpu.SMEM)] + [hbm] * 8,
        out_specs=(hbm,) * 3,
        scratch_shapes=[
            pltpu.VMEM((slices, tall * PITCH, LANES), f32),
            pltpu.VMEM((slices, tall * PITCH, LANES), f32),
            pltpu.SMEM((patterns.shape[0],), jnp.int32),
        ]
        + [
            pltpu.VMEM(x.shape, x.dtype)
            for x in (own, up, down, west, east, probe, patterns, tables)
        ]
        + [
            pltpu.VMEM((slices, tall, tile_x), f32),
            pltpu.VMEM((slices, tall, half), bf16),
            pltpu.VMEM((slices, tall, half), bf16),
            pltpu.SemaphoreType.DMA((8,)),
            pltpu.SemaphoreType.DMA((slices, 3)),
        ]
        + [
            pltpu.VMEM((GROUP, slices, 2, width, width), f32),
            pltpu.VMEM((GROUP, slices, 2, width, width), f32),
            pltpu.VMEM((2 * width, GROUP * width), bf16),
            pltpu.VMEM((GROUP * width, 2 * width), bf16),
        ]
        * STREAMS,
        compiler_params=pltpu.CompilerParams(vmem_limit_bytes=56 << 20),
        interpret=interpret,
    )(where, own, up, down, west, east, probe, patterns, tables)


def parcel_kernel(centers_ref, pat_ref, sent_ref):
    slots, _, width = sent_ref.shape
    bf16 = jnp.bfloat16
    lane = lax.broadcasted_iota(jnp.int32, (SLOT_PAD, width), 1)
    sent_ref[...] = jnp.zeros(sent_ref.shape, bf16)
    for p in range(pat_ref.shape[0]):
        owner = centers_ref[p, 1] // TILE
        row = centers_ref[p, 0] % TILE
        col = centers_ref[p, 1] % TILE
        info = jnp.where(lane == 0, row, jnp.where(lane == 1, col, jnp.where(lane == 2, 1, 0)))
        sent_ref[owner, :width] = pat_ref[p]
        sent_ref[owner, width:] = info.astype(jnp.float32).astype(bf16)


def parcels(centers, patterns, slots):
    width = patterns.shape[1]
    vmem = pl.BlockSpec(memory_space=pltpu.VMEM)
    return pl.pallas_call(
        parcel_kernel,
        out_shape=jax.ShapeDtypeStruct((slots, width + SLOT_PAD, width), jnp.bfloat16),
        in_specs=[pl.BlockSpec(memory_space=pltpu.SMEM), vmem],
        out_specs=vmem,
        compiler_params=pltpu.CompilerParams(vmem_limit_bytes=56 << 20),
    )(centers, patterns)


def shift(cells, axis, step):
    count = lax.axis_size(axis)
    pairs = [(i, i + step) for i in range(count) if 0 <= i + step < count]
    return lax.ppermute(cells, axis, pairs)


def per_device(tables, potential, probe, patterns, scan_centers):
    slices, tile_y, tile_x = potential.shape
    width = probe.shape[1]
    half = width // 2
    columns = lax.axis_size("tx")
    f32, bf16 = jnp.float32, jnp.bfloat16

    rounded = potential.astype(bf16)
    up = shift(rounded[:, tile_y - half :], "ty", 1)
    down = shift(rounded[:, :half], "ty", -1)

    sent = parcels(scan_centers, patterns, columns)
    got = lax.all_to_all(sent, "tx", split_axis=0, concat_axis=0, tiled=True)
    where = got[:, width, :3].astype(f32).astype(jnp.int32)

    def strip(cols):
        return jnp.concatenate([up[:, :, cols], rounded[:, :, cols], down[:, :, cols]], 1)

    west = shift(strip(slice(tile_x - half, tile_x)), "tx", 1)
    east = shift(strip(slice(0, half)), "tx", -1)

    mid, to_west, to_east = run_windows(
        where, potential, up, down, west, east, probe, got, tables
    )

    from_west = shift(to_east, "tx", 1)
    from_east = shift(to_west, "tx", -1)

    def with_sides(lo, hi):
        add = jnp.concatenate([from_west[:, lo:hi], from_east[:, lo:hi]], 2)
        return mid[:, lo:hi] + add.astype(f32)

    from_up = shift(with_sides(half + tile_y, 2 * half + tile_y).astype(bf16), "ty", 1)
    from_down = shift(with_sides(0, half).astype(bf16), "ty", -1)
    return with_sides(half, half + tile_y) + jnp.concatenate([from_up, from_down], 1).astype(f32)


def solution(mesh):
    in_specs = (P(None, "ty", "tx"), P(), P(("ty", "tx"), None, None), P(("ty", "tx"), None))
    out_specs = P(None, "ty", "tx")

    def run(potential, probe, patterns, scan_centers):
        tables = jnp.asarray(make_tables(probe.shape[1]))
        return jax.shard_map(
            functools.partial(per_device, tables),
            mesh=mesh, in_specs=in_specs, out_specs=out_specs, check_vma=False,
        )(potential, probe, patterns, scan_centers)

    return run
```

```python
import functools
import math

import jax
import jax.numpy as jnp
import numpy as np
from jax import lax
from jax.experimental import pallas as pl
from jax.experimental.pallas import tpu as pltpu
from jax.sharding import PartitionSpec as P

fresnel = 41.0
band_reach = 20.0
SLOT_PAD = 16
TILE = 256
LANES = 128
PITCH = 5
GROUP = 2
STREAMS = 2


def sin_cos_coefs(limit):
    nodes = np.cos((np.arange(512) + 0.5) * np.pi / 512)
    u = 0.5 * (nodes + 1.0)
    v = np.sqrt(u) * limit
    t = 0.25 * v
    scale = limit * limit
    a = np.polynomial.polynomial.polyfit(u, 2 * np.sin(t) / v, 4) / scale ** np.arange(5)
    b = np.polynomial.polynomial.polyfit(u, np.cos(t), 4) / scale ** np.arange(5)
    return [float(np.float32(x)) for x in a], [float(np.float32(x)) for x in b]


SIN_COEFS, COS_COEFS = sin_cos_coefs(6.0)


def sin_cos_half(v):
    u = v * v
    s = SIN_COEFS[-1]
    for a in SIN_COEFS[-2::-1]:
        s = s * u + a
    c = COS_COEFS[-1]
    for b in COS_COEFS[-2::-1]:
        c = c * u + b
    s = s * v
    return s * c, 1.0 - 0.5 * (s * s)


def make_tables(length):
    f32 = np.float32
    indices = np.arange(length, dtype=np.int32)
    gap = (indices[:, None] - indices[None, :]).astype(f32)
    chirp = f32(math.pi) * gap * gap / f32(fresnel)
    amplitude = (np.abs(gap) <= band_reach).astype(f32) / f32(math.sqrt(fresnel))
    product = indices[:, None] * indices[None, :] % length
    angle = f32(-2.0 * math.pi) * product.astype(f32) / f32(length)
    norm = f32(1.0 / math.sqrt(length))
    pairs = [
        (amplitude * np.cos(chirp), amplitude * np.sin(chirp)),
        (np.cos(angle) * norm, np.sin(angle) * norm),
    ]
    tables = []
    for re, im in pairs:
        left = np.block([[re, -im], [im, re]])
        right = np.block([[re, im], [-im, re]])
        tables += [left.astype(jnp.bfloat16), right.astype(jnp.bfloat16)]
    return np.stack(tables)


def windows_kernel(
    half, where_ref, own_hbm, up_hbm, down_hbm, west_hbm, east_hbm, probe_hbm, tab_hbm, *refs,
):
    slots = where_ref.shape[0]
    pat_hbms = refs[:slots]
    mid_hbm, wout_hbm, eout_hbm = refs[slots : slots + 3]
    (
        ext_ref, acc_ref, order_ref, own_ref, up_ref, down_ref, west_ref, east_ref, probe_ref, pat_ref,
        tab_ref, mid_ref, wout_ref, eout_ref, in_sems, out_sems, *streams,
    ) = refs[slots + 3 :]
    sources = (west_hbm, east_hbm, up_hbm, down_hbm, own_hbm, tab_hbm, probe_hbm) + pat_hbms
    targets = (west_ref, east_ref, up_ref, down_ref, own_ref, tab_ref, probe_ref)
    targets += tuple(pat_ref.at[k] for k in range(slots))
    loads = [
        pltpu.make_async_copy(source, into, in_sems.at[i])
        for i, (source, into) in enumerate(zip(sources, targets))
    ]
    for load in loads:
        load.start()
    slices, tile_y, tile_x = own_ref.shape
    width = probe_ref.shape[1]
    rows = 64
    f32, bf16 = jnp.float32, jnp.bfloat16
    tall = tile_y + width
    blocks = (tile_x + width) // LANES
    side = half // LANES
    halves = width // LANES

    def every(start, count, block):
        return pl.ds(start * PITCH + block, count, stride=PITCH)

    for s in range(slices):
        acc_ref[s] = jnp.zeros(acc_ref.shape[1:], f32)
    for load in loads[:2]:
        load.wait()
    for s in range(slices):
        for c in range(side):
            lanes = slice(c * LANES, (c + 1) * LANES)
            ext_ref[s, every(0, tall, c)] = west_ref[s, :, lanes].astype(f32)
            ext_ref[s, every(0, tall, blocks - side + c)] = east_ref[s, :, lanes].astype(f32)
    for load in loads[2:5]:
        load.wait()
    for s in range(slices):
        for c in range(blocks - 2 * side):
            lanes = slice(c * LANES, (c + 1) * LANES)
            ext_ref[s, every(0, half, side + c)] = up_ref[s, :, lanes].astype(f32)
            ext_ref[s, every(half + tile_y, half, side + c)] = down_ref[s, :, lanes].astype(f32)
            ext_ref[s, every(half, tile_y, side + c)] = own_ref[s, :, lanes].astype(bf16).astype(f32)
    for load in loads[5:]:
        load.wait()

    def dot(a, b):
        return jnp.dot(a, b, preferred_element_type=f32)

    def chunks():
        return [slice(k * rows, (k + 1) * rows) for k in range(width // rows)]

    def group(slot_list, cs_ref, phi_ref, s_ref, t_ref):
        places = []
        lane = lax.broadcasted_iota(jnp.int32, (rows, LANES), 1)
        for slot in slot_list:
            row = where_ref[slot, 0]
            col = where_ref[slot, 1]
            block = col // LANES
            turn = col - block * LANES
            back = jnp.where(turn == 0, 0, LANES - turn)
            weight = jnp.where(where_ref[slot, 2] > 0, 1.0, 0.0)
            places.append((row, block, turn, back, lane < LANES - turn, lane >= turn, weight))

        def modulate(w, s, k, re, im):
            row, block, turn, back, low, high, weight = places[w]
            parts = [
                pltpu.roll(ext_ref[s, every(row + k.start, rows, block + j)], back, 1)
                for j in range(halves + 1)
            ]
            for j in range(halves):
                c = slice(j * LANES, (j + 1) * LANES)
                into = slice(w * width + c.start, w * width + c.stop)
                sin, cos = sin_cos_half(jnp.where(low, parts[j], parts[j + 1]))
                new_re = re[:, c] * cos - im[:, c] * sin
                new_im = re[:, c] * sin + im[:, c] * cos
                if s:
                    cs_ref[w, s, 0, k, c] = cos
                    cs_ref[w, s, 1, k, c] = sin
                phi_ref[w, s, 0, k, c] = new_re
                phi_ref[w, s, 1, k, c] = new_im
                s_ref[k, into] = new_re.astype(bf16)
                s_ref[width + k.start : width + k.stop, into] = new_im.astype(bf16)

        def deposit(w, s, k, grad):
            row, block, turn, back, low, high, weight = places[w]
            parts = [pltpu.roll(grad[:, j * LANES : (j + 1) * LANES], turn, 1) for j in range(halves)]
            zero = jnp.zeros((rows, LANES), f32)
            for j in range(halves + 1):
                here = parts[j] if j < halves else zero
                before = parts[j - 1] if j else zero
                acc_ref[s, every(row + k.start, rows, block + j)] += jnp.where(high, here, before)

        def span(w):
            return slice(w * width, (w + 1) * width)

        def left(table):
            return dot(tab_ref[table], s_ref[...])

        def right(table):
            return dot(t_ref[...], tab_ref[table])

        many = range(len(slot_list))
        for w in many:
            for k in chunks():
                modulate(w, 0, k, probe_ref[0, k], probe_ref[1, k])
        for s in range(1, slices + 1):
            table = 2 if s == slices else 0
            yield
            mid = left(table).astype(bf16)
            for w in many:
                t_ref[span(w), :width] = mid[:width, span(w)]
                t_ref[span(w), width:] = mid[width:, span(w)]
            z = right(table + 1)
            yield
            for w in many:
                for k in chunks():
                    own = slice(w * width + k.start, w * width + k.stop)
                    re, im = z[own, :width], z[own, width:]
                    if s < slices:
                        modulate(w, s, k, re, im)
                    else:
                        excess = re * re + im * im - pat_ref[slot_list[w], k].astype(f32)
                        t_ref[own, :width] = (excess * re).astype(bf16)
                        t_ref[own, width:] = (excess * im).astype(bf16)
        for s in range(slices - 1, -1, -1):
            table = 2 if s == slices - 1 else 0
            yield
            mid = right(table).astype(bf16)
            for w in many:
                s_ref[:width, span(w)] = mid[span(w), :width]
                s_ref[width:, span(w)] = mid[span(w), width:]
            g = left(table + 1)
            yield
            for w in many:
                for k in chunks():
                    own = slice(w * width + k.start, w * width + k.stop)
                    re, im = g[k, span(w)], g[width + k.start : width + k.stop, span(w)]
                    grad = places[w][-1] * (im * phi_ref[w, s, 0, k] - re * phi_ref[w, s, 1, k])
                    deposit(w, s, k, grad)
                    if s:
                        cos, sin = cs_ref[w, s, 0, k], cs_ref[w, s, 1, k]
                        t_ref[own, :width] = (re * cos + im * sin).astype(bf16)
                        t_ref[own, width:] = (im * cos - re * sin).astype(bf16)

    def list_slots(wanted):
        def body(slot, count):
            filled = where_ref[slot, 2] > 0

            @pl.when(filled == wanted)
            def _():
                order_ref[count] = slot

            return count + jnp.where(filled == wanted, 1, 0)

        return body

    filled = lax.fori_loop(0, slots, list_slots(True), 0)
    lax.fori_loop(0, slots, list_slots(False), filled)
    batch = STREAMS * GROUP

    def many_windows(number, carry):
        running = []
        for i in range(STREAMS):
            base = number * batch + i * GROUP
            chosen = [order_ref[base + w] for w in range(GROUP)]
            running.append(group(chosen, *streams[4 * i : 4 * i + 4]))
        for i, stream in enumerate(running):
            for _ in range(STREAMS - 1 - i):
                next(stream)
        alive = True
        while alive:
            alive = False
            for stream in running:
                alive = next(stream, True) is None or alive
        return carry

    lax.fori_loop(0, (filled + batch - 1) // batch, many_windows, 0)

    stores = []
    for s in range(slices):
        for b in range(blocks):
            part = acc_ref[s, every(0, tall, b)]
            if b < side:
                wout_ref[s, :, b * LANES : (b + 1) * LANES] = part.astype(bf16)
            elif b >= blocks - side:
                c = b - (blocks - side)
                eout_ref[s, :, c * LANES : (c + 1) * LANES] = part.astype(bf16)
            else:
                c = b - side
                mid_ref[s, :, c * LANES : (c + 1) * LANES] = part
        for j, (source, into) in enumerate(
            ((mid_ref, mid_hbm), (wout_ref, wout_hbm), (eout_ref, eout_hbm))
        ):
            stores.append(pltpu.make_async_copy(source.at[s], into.at[s], out_sems.at[s, j]))
            stores[-1].start()
    for store in stores:
        store.wait()


def run_windows(where, own, up, down, west, east, probe, patterns, tables, interpret=False):
    slices, tile_y, tile_x = own.shape
    width = probe.shape[1]
    slots = len(patterns)
    half = width // 2
    tall = tile_y + width
    f32, bf16 = jnp.float32, jnp.bfloat16
    hbm = pl.BlockSpec(memory_space=pltpu.HBM)
    return pl.pallas_call(
        functools.partial(windows_kernel, half),
        out_shape=(
            jax.ShapeDtypeStruct((slices, tall, tile_x), f32),
            jax.ShapeDtypeStruct((slices, tall, half), bf16),
            jax.ShapeDtypeStruct((slices, tall, half), bf16),
        ),
        in_specs=[pl.BlockSpec(memory_space=pltpu.SMEM)] + [hbm] * (7 + slots),
        out_specs=(hbm,) * 3,
        scratch_shapes=[
            pltpu.VMEM((slices, tall * PITCH, LANES), f32),
            pltpu.VMEM((slices, tall * PITCH, LANES), f32),
            pltpu.SMEM((slots,), jnp.int32),
        ]
        + [
            pltpu.VMEM(x.shape, x.dtype) for x in (own, up, down, west, east, probe)
        ]
        + [pltpu.VMEM((slots,) + patterns[0].shape, bf16), pltpu.VMEM(tables.shape, bf16)]
        + [
            pltpu.VMEM((slices, tall, tile_x), f32),
            pltpu.VMEM((slices, tall, half), bf16),
            pltpu.VMEM((slices, tall, half), bf16),
            pltpu.SemaphoreType.DMA((7 + slots,)),
            pltpu.SemaphoreType.DMA((slices, 3)),
        ]
        + [
            pltpu.VMEM((GROUP, slices, 2, width, width), f32),
            pltpu.VMEM((GROUP, slices, 2, width, width), f32),
            pltpu.VMEM((2 * width, GROUP * width), bf16),
            pltpu.VMEM((GROUP * width, 2 * width), bf16),
        ]
        * STREAMS,
        compiler_params=pltpu.CompilerParams(vmem_limit_bytes=56 << 20),
        interpret=interpret,
    )(where, own, up, down, west, east, probe, tables, *patterns)


def parcel_kernel(me_ref, centers_ref, pat_ref, *sent_refs):
    slots, width = len(sent_refs), pat_ref.shape[1]
    count = pat_ref.shape[0]
    lane = lax.broadcasted_iota(jnp.int32, (SLOT_PAD, width), 1)
    steps, infos = [], []
    for p in range(count):
        steps.append(lax.rem(centers_ref[p, 1] // TILE - me_ref[0] + slots, slots))
        row = centers_ref[p, 0] % TILE
        col = centers_ref[p, 1] % TILE
        info = jnp.where(lane == 0, row, jnp.where(lane == 1, col, jnp.where(lane == 2, 1, 0)))
        infos.append(info.astype(jnp.float32).astype(jnp.bfloat16))
    for k in range(slots):
        sent_refs[k][...] = jnp.zeros(sent_refs[k].shape, jnp.bfloat16)
        for p in range(count):

            @pl.when(steps[p] == k)
            def _(k=k, p=p):
                sent_refs[k][:width] = pat_ref[p]
                sent_refs[k][width:] = infos[p]


def parcels(me, centers, patterns, slots):
    width = patterns.shape[1]
    vmem = pl.BlockSpec(memory_space=pltpu.VMEM)
    smem = pl.BlockSpec(memory_space=pltpu.SMEM)
    parcel = jax.ShapeDtypeStruct((width + SLOT_PAD, width), jnp.bfloat16)
    return pl.pallas_call(
        parcel_kernel,
        out_shape=(parcel,) * slots,
        in_specs=[smem, smem, vmem],
        out_specs=(vmem,) * slots,
        compiler_params=pltpu.CompilerParams(vmem_limit_bytes=56 << 20),
    )(me, centers, patterns)


def shift(cells, axis, step):
    count = lax.axis_size(axis)
    pairs = [(i, i + step) for i in range(count) if 0 <= i + step < count]
    return lax.ppermute(cells, axis, pairs)


def per_device(tables, potential, probe, patterns, scan_centers):
    slices, tile_y, tile_x = potential.shape
    width = probe.shape[1]
    half = width // 2
    columns = lax.axis_size("tx")
    f32, bf16 = jnp.float32, jnp.bfloat16

    rounded = potential.astype(bf16)
    up = shift(rounded[:, tile_y - half :], "ty", 1)
    down = shift(rounded[:, :half], "ty", -1)

    me = lax.axis_index("tx").astype(jnp.int32)[None]
    got = [
        parcel if k == 0 else lax.ppermute(parcel, "tx", [(i, (i + k) % columns) for i in range(columns)])
        for k, parcel in enumerate(parcels(me, scan_centers, patterns, columns))
    ]
    where = jnp.stack([parcel[width, :3] for parcel in got]).astype(f32).astype(jnp.int32)

    def strip(cols):
        return jnp.concatenate([up[:, :, cols], rounded[:, :, cols], down[:, :, cols]], 1)

    west = shift(strip(slice(tile_x - half, tile_x)), "tx", 1)
    east = shift(strip(slice(0, half)), "tx", -1)

    mid, to_west, to_east = run_windows(
        where, potential, up, down, west, east, probe, got, tables
    )

    from_west = shift(to_east, "tx", 1)
    from_east = shift(to_west, "tx", -1)

    def with_sides(lo, hi):
        add = jnp.concatenate([from_west[:, lo:hi], from_east[:, lo:hi]], 2)
        return mid[:, lo:hi] + add.astype(f32)

    from_up = shift(with_sides(half + tile_y, 2 * half + tile_y).astype(bf16), "ty", 1)
    from_down = shift(with_sides(0, half).astype(bf16), "ty", -1)
    return with_sides(half, half + tile_y) + jnp.concatenate([from_up, from_down], 1).astype(f32)


def solution(mesh):
    in_specs = (P(None, "ty", "tx"), P(), P(("ty", "tx"), None, None), P(("ty", "tx"), None))
    out_specs = P(None, "ty", "tx")

    def run(potential, probe, patterns, scan_centers):
        tables = jnp.asarray(make_tables(probe.shape[1]))
        return jax.shard_map(
            functools.partial(per_device, tables),
            mesh=mesh, in_specs=in_specs, out_specs=out_specs, check_vma=False,
        )(potential, probe, patterns, scan_centers)

    return run
```
